128 devices in a mesh: lat: 8 (over x, z_hi), lon: 16 (over z_lo, y, core).
Axes of the slice: x: 4, y: 4, z: 4 (z_hi: 2, z_lo: 2; z = z_hi * 2 + z_lo), core: 2. Of those that a mesh axis runs over, the one named last changes fastest.
Arguments:
- fine_field: bfloat16 [4, 96, 192, 512], P(None, 'lat', 'lon'), may hold values from -6 to 6
- offsets: int32 [4], replicated, may hold values from 1 to 11, as said below
- fine_prenorm: float32 [512], replicated, may hold values from 0.25 to 1.75
- fine_triple: bfloat16 [512, 1536], replicated, may hold values from -0.25 to 0.25
- fine_bias: float32 [16, 144, 144], replicated, may hold values from -160 to 160
- fine_output: bfloat16 [512, 512], replicated, may hold values from -0.25 to 0.25
- fine_midnorm: float32 [512], replicated, may hold values from 0.25 to 1.75
- fine_expand: bfloat16 [512, 2048], replicated, may hold values from -0.25 to 0.25
- fine_reduce: bfloat16 [2048, 512], replicated, may hold values from -0.125 to 0.125
- merge_gain: float32 [2048], replicated, may hold values from 0.25 to 1.75
- merge_weight: bfloat16 [2048, 1024], replicated, may hold values from -0.125 to 0.125
- coarse_prenorm: float32 [1024], replicated, may hold values from 0.25 to 1.75
- coarse_triple: bfloat16 [1024, 3072], P(None, 'lon'), may hold values from -0.1875 to 0.1875
- coarse_bias: float32 [32, 144, 144], P('lon'), may hold values from -160 to 160
- coarse_output: bfloat16 [1024, 1024], P('lon'), may hold values from -0.1875 to 0.1875
- coarse_midnorm: float32 [1024], replicated, may hold values from 0.25 to 1.75
- coarse_expand: bfloat16 [1024, 4096], P(None, 'lon'), may hold values from -0.1875 to 0.1875
- coarse_reduce: bfloat16 [4096, 1024], P('lon'), may hold values from -0.09375 to 0.09375
- upsample_weight: bfloat16 [1024, 2048], replicated, may hold values from -0.1875 to 0.1875
Outputs:
- blended: bfloat16 [4, 96, 192, 512], P(None, 'lat', 'lon')
- coarse_state: bfloat16 [4, 48, 96, 1024], P(None, 'lat', 'lon')
The draws below stay inside these ranges and needn't reach their ends.
Inputs may be any that keep to these rules, and one draw needn't show every extreme that they name: `offsets`: entries 0 and 2 lie in 1 to 5, entries 1 and 3 in 1 to 11; in every draw entry 0 or entry 2 equals 5, and entry 1 or entry 3 equals 11.
All inputs are finite; a program needn't handle non-finite values.
Results may differ from the reference program's by a relative error of at most 0.024.
Values may be sent and summed in bfloat16 or wider, within the bound.
No kernel may reach another device: no remote copies, remote signals or barrier semaphores. Data moves between devices by JAX's collectives and lax.ppermute only.
A program may use at most 128 MiB of HBM per device.

```python
import jax
import jax.numpy as jnp
from jax import lax

C1 = 512
H1 = 16
C2 = 1024
H2 = 32
DEP = 4
WD = 2
WL = 6
WW = 12
WT = 144
FF1 = 2048
FF2 = 4096
HF = 96
WG = 192
WC = 96
N_LON = 16


def pair_score_table(key, head_count):
    base_vals = jnp.clip(jax.random.normal(key, (head_count, WT, WT), jnp.float32), -4.0, 4.0)
    return base_vals


def draw_fine_bias(key, part):
    return pair_score_table(jax.random.fold_in(key, 11), H1)


def draw_coarse_bias(key, part):
    return pair_score_table(jax.random.fold_in(key, 13), H2)


def draw_offsets(key, part):
    key_list = jax.random.split(jax.random.fold_in(key, 3), 4)
    lat_other = jax.random.randint(key_list[0], (), 1, WL)
    lon_other = jax.random.randint(key_list[1], (), 1, WW)
    lat_side = jax.random.randint(key_list[2], (), 0, 2)
    lon_side = jax.random.randint(key_list[3], (), 0, 2)
    lat_most = jnp.full((), WL - 1, jnp.int32)
    lon_most = jnp.full((), WW - 1, jnp.int32)
    fine_lat = jnp.where(lat_side == 0, lat_most, lat_other)
    coarse_lat = jnp.where(lat_side == 0, lat_other, lat_most)
    fine_lon = jnp.where(lon_side == 0, lon_most, lon_other)
    coarse_lon = jnp.where(lon_side == 0, lon_other, lon_most)
    return jnp.stack([fine_lat, fine_lon, coarse_lat, coarse_lon]).astype(jnp.int32)


def shard_levels(rng, extent, shards, low, high):
    factor_of = 1.0
    for position, shards_of in shards:
        heights = jax.random.uniform(jax.random.fold_in(jax.random.fold_in(rng, 6), position), (shards_of,), jnp.float32, low / len(shards), high / len(shards))
        factor_of = factor_of * jnp.repeat(jnp.exp(heights), extent[position] // shards_of).reshape((-1,) + (1,) * (len(extent) - 1 - position))
    return factor_of


def gaussian(rng, shape, scale, limit, cuts=(), kind=jnp.bfloat16):
    level = shard_levels(rng, shape, cuts, -0.22, 0.18) if cuts else 1.0
    drawn = jax.random.normal(rng, shape, jnp.float32) * scale * level
    return jnp.minimum(jnp.maximum(drawn, -limit), limit).astype(kind)


def setup_inputs(seed: int = 0) -> dict:
    arg_keys = jax.random.split(jax.random.key(seed), 20)
    fine_field = gaussian(arg_keys[0], (DEP, HF, WG, C1), 1.0, 6.0, ((1, 8), (2, 16)))
    offsets = draw_offsets(jax.random.fold_in(arg_keys[19], 71), 0)
    fine_prenorm = jnp.clip(1.0 + 0.15 * jax.random.normal(arg_keys[2], (C1,), jnp.float32), 0.25, 1.75)
    fine_triple = gaussian(arg_keys[3], (C1, 3 * C1), C1 ** -0.5, 0.25)
    fine_bias = draw_fine_bias(jax.random.fold_in(arg_keys[19], 71), 0)
    fine_output = gaussian(arg_keys[5], (C1, C1), C1 ** -0.5, 0.25)
    fine_midnorm = jnp.clip(1.0 + 0.15 * jax.random.normal(arg_keys[6], (C1,), jnp.float32), 0.25, 1.75)
    fine_expand = gaussian(arg_keys[7], (C1, FF1), C1 ** -0.5, 0.25)
    fine_reduce = gaussian(arg_keys[8], (FF1, C1), FF1 ** -0.5, 0.125)
    merge_gain = jnp.clip(1.0 + 0.15 * jax.random.normal(arg_keys[9], (4 * C1,), jnp.float32), 0.25, 1.75)
    merge_weight = gaussian(arg_keys[10], (4 * C1, C2), (4 * C1) ** -0.5, 0.125)
    coarse_prenorm = jnp.clip(1.0 + 0.15 * jax.random.normal(arg_keys[11], (C2,), jnp.float32), 0.25, 1.75)
    coarse_triple = gaussian(arg_keys[12], (C2, 3 * C2), C2 ** -0.5, 0.1875, ((1, 16),))
    coarse_bias = draw_coarse_bias(jax.random.fold_in(arg_keys[19], 71), 0)
    coarse_output = gaussian(arg_keys[14], (C2, C2), C2 ** -0.5, 0.1875, ((0, 16),))
    coarse_midnorm = jnp.clip(1.0 + 0.15 * jax.random.normal(arg_keys[15], (C2,), jnp.float32), 0.25, 1.75)
    coarse_expand = gaussian(arg_keys[16], (C2, FF2), C2 ** -0.5, 0.1875, ((1, 16),))
    coarse_reduce = gaussian(arg_keys[17], (FF2, C2), FF2 ** -0.5, 0.09375, ((0, 16),))
    upsample_weight = gaussian(arg_keys[18], (C2, 4 * C1), C2 ** -0.5, 0.1875)
    return dict(fine_field=fine_field, offsets=offsets, fine_prenorm=fine_prenorm, fine_triple=fine_triple, fine_bias=fine_bias, fine_output=fine_output, fine_midnorm=fine_midnorm, fine_expand=fine_expand, fine_reduce=fine_reduce, merge_gain=merge_gain, merge_weight=merge_weight, coarse_prenorm=coarse_prenorm, coarse_triple=coarse_triple, coarse_bias=coarse_bias, coarse_output=coarse_output, coarse_midnorm=coarse_midnorm, coarse_expand=coarse_expand, coarse_reduce=coarse_reduce, upsample_weight=upsample_weight)


epsilon = 1e-05
masked_score = -1e+30

def layer_norm(values, gain_vec):
    values = values.astype(jnp.float32)
    center = lax.optimization_barrier(jnp.mean(values, axis=-1, keepdims=True))
    offset_vals = values - center
    spread = lax.optimization_barrier(jnp.mean(offset_vals * offset_vals, axis=-1, keepdims=True))
    return offset_vals * lax.rsqrt(spread + epsilon) * gain_vec

def to_windows(cells_grid):
    levels, lat_rows, lon_cols, channels = cells_grid.shape
    shaped = cells_grid.reshape(levels // WD, WD, lat_rows // WL, WL, lon_cols // WW, WW, channels)
    shaped = shaped.transpose(0, 2, 4, 1, 3, 5, 6)
    return shaped.reshape(-1, WT, channels)

def from_windows(windows, levels, lat_rows, lon_cols):
    channels = windows.shape[-1]
    shaped = windows.reshape(levels // WD, lat_rows // WL, lon_cols // WW, WD, WL, WW, channels)
    return shaped.transpose(0, 3, 1, 4, 2, 5, 6).reshape(levels, lat_rows, lon_cols, channels)

def window_mix(triples, regions, bias_table):
    count_win = triples.shape[0]
    heads_all = bias_table.shape[0]
    head_dim = triples.shape[-1] // (3 * heads_all)
    parts_all = triples.astype(jnp.float32).reshape(count_win, WT, heads_all, 3, head_dim)
    queries = parts_all[:, :, :, 0]
    keys_all = parts_all[:, :, :, 1]
    values = parts_all[:, :, :, 2]
    scores = jnp.einsum('nihd,njhd->nhij', queries, keys_all) * head_dim ** (-0.5) + bias_table[None]
    allowed = regions[:, :, None] == regions[:, None, :]
    scores = jnp.where(allowed[:, None], scores, masked_score)
    row_top = lax.optimization_barrier(jnp.max(scores, axis=-1, keepdims=True))
    lifted = jnp.exp(scores - row_top)
    weights = (lifted / lax.optimization_barrier(jnp.sum(lifted, axis=-1, keepdims=True))).astype(jnp.bfloat16)
    mixed_out = jnp.einsum('nhij,njhd->nihd', weights.astype(jnp.float32), values)
    return mixed_out.astype(jnp.bfloat16).reshape(count_win, WT, heads_all * head_dim)

def shifted_attention(normed, shift_lat, shift_lon, triple_weight, bias_table):
    levels, lat_rows, lon_cols, channels = normed.shape
    rolled = jnp.roll(normed, (-shift_lat, -shift_lon), axis=(1, 2))
    triples = jnp.dot(rolled.reshape(-1, channels), triple_weight, preferred_element_type=jnp.float32).astype(jnp.bfloat16)
    triples = to_windows(triples.reshape(levels, lat_rows, lon_cols, -1))
    anchor = (jnp.arange(lat_rows, dtype=jnp.int32) + shift_lat) % lat_rows
    regions = jnp.broadcast_to((anchor < shift_lat).astype(jnp.int32)[None, :, None, None], (levels, lat_rows, lon_cols, 1))
    regions = to_windows(regions)[:, :, 0]
    item_count = levels // WD * (lat_rows // WL)
    mixed_out = lax.map(lambda operands: window_mix(operands[0], operands[1], bias_table), (triples.reshape(item_count, -1, WT, triples.shape[-1]), regions.reshape(item_count, -1, WT)))
    mixed_out = from_windows(mixed_out.reshape(-1, WT, mixed_out.shape[-1]), levels, lat_rows, lon_cols)
    return jnp.roll(mixed_out, (shift_lat, shift_lon), axis=(1, 2))

def grouped_sum(operand, weight, groups):
    inner_dim = operand.shape[-1]
    outer_dim = weight.shape[-1]
    split_weight = weight.astype(jnp.float32).reshape(groups, inner_dim // groups, outer_dim)

    def one_block(token_block):
        shaped = token_block.astype(jnp.float32).reshape(token_block.shape[0], groups, inner_dim // groups)
        partials = jnp.einsum('tgk,gkn->tgn', shaped, split_weight).astype(jnp.bfloat16)
        return lax.optimization_barrier(jnp.sum(partials.astype(jnp.float32), axis=1))
    blocks = operand.reshape(-1, WC, inner_dim)
    return lax.map(one_block, blocks).reshape(-1, outer_dim)

def reference(fine_field, offsets, fine_prenorm, fine_triple, fine_bias, fine_output, fine_midnorm, fine_expand, fine_reduce, merge_gain, merge_weight, coarse_prenorm, coarse_triple, coarse_bias, coarse_output, coarse_midnorm, coarse_expand, coarse_reduce, upsample_weight):
    levels, lat_rows, lon_cols, channels = fine_field.shape
    normed = layer_norm(fine_field, fine_prenorm).astype(jnp.bfloat16)
    mixed_out = shifted_attention(normed, offsets[0], offsets[1], fine_triple, fine_bias)
    attended = (fine_field.astype(jnp.float32).reshape(-1, channels) + jnp.dot(mixed_out.reshape(-1, channels), fine_output, preferred_element_type=jnp.float32)).astype(jnp.bfloat16)
    hidden = jax.nn.gelu(jnp.dot(layer_norm(attended, fine_midnorm).astype(jnp.bfloat16), fine_expand, preferred_element_type=jnp.float32)).astype(jnp.bfloat16)
    fine_state = (attended.astype(jnp.float32) + jnp.dot(hidden, fine_reduce, preferred_element_type=jnp.float32)).astype(jnp.bfloat16)
    fine_state = fine_state.reshape(levels, lat_rows, lon_cols, channels)
    half_rows = lat_rows // 2
    half_cols = lon_cols // 2
    merged = fine_state.reshape(levels, half_rows, 2, half_cols, 2, channels).transpose(0, 1, 3, 4, 2, 5)
    merged = merged.reshape(-1, 4 * channels)
    coarse_in = jnp.dot(layer_norm(merged, merge_gain).astype(jnp.bfloat16), merge_weight, preferred_element_type=jnp.float32).astype(jnp.bfloat16)
    wide_channels = coarse_in.shape[-1]
    normed2 = layer_norm(coarse_in, coarse_prenorm).astype(jnp.bfloat16).reshape(levels, half_rows, half_cols, wide_channels)
    mixed2 = shifted_attention(normed2, offsets[2], offsets[3], coarse_triple, coarse_bias)
    coarse_mid = (coarse_in.astype(jnp.float32) + grouped_sum(mixed2.reshape(-1, wide_channels), coarse_output, N_LON)).astype(jnp.bfloat16)
    hidden2 = jax.nn.gelu(jnp.dot(layer_norm(coarse_mid, coarse_midnorm).astype(jnp.bfloat16), coarse_expand, preferred_element_type=jnp.float32)).astype(jnp.bfloat16)
    coarse_state = (coarse_mid.astype(jnp.float32) + grouped_sum(hidden2, coarse_reduce, N_LON)).astype(jnp.bfloat16)
    expanded = jnp.dot(coarse_state, upsample_weight, preferred_element_type=jnp.float32).reshape(levels, half_rows, half_cols, 2, 2, channels)
    expanded = expanded.transpose(0, 1, 4, 2, 3, 5).reshape(levels, lat_rows, lon_cols, channels)
    blended = (fine_state.astype(jnp.float32) + expanded).astype(jnp.bfloat16)
    return (blended, coarse_state.reshape(levels, half_rows, half_cols, wide_channels))
```

```python
import jax
import jax.numpy as jnp
from jax import lax
from jax.sharding import PartitionSpec as P
from jax.experimental import pallas as pl
from jax.experimental.pallas import tpu as pltpu

BF = jnp.bfloat16
F32 = jnp.float32
EPS = 1e-05
NEG = -1e30
WT = 144
VLIM = 56 * 1024 * 1024


def full_spec(n, smem=()):
    return [
        pl.BlockSpec(memory_space=pltpu.SMEM) if i in smem else pl.BlockSpec(memory_space=pltpu.VMEM)
        for i in range(n)
    ]


def norm_rows(x, gain):
    mean = jnp.mean(x, axis=-1, keepdims=True)
    off = x - mean
    var = jnp.mean(off * off, axis=-1, keepdims=True)
    return off * lax.rsqrt(var + EPS) * gain


def dot_nt(a, b):
    return lax.dot_general(a, b, (((1,), (1,)), ((), ())), preferred_element_type=F32)


def dot_nn(a, b):
    return jnp.dot(a, b, preferred_element_type=F32)


def rows_to_tiles(rows, tiles, first):
    count = rows.shape[0]
    for c in range(8):
        tiles[pl.ds(first * 8 + c, count, stride=8), :] = rows[:, 128 * c : 128 * c + 128]


def tiles_to_rows(tiles, first, count):
    return [tiles[pl.ds(first * 8 + c, count, stride=8), :] for c in range(8)]


def attend_group(q, k, v, bias_of, extra, scale, store):
    lane_head = lax.broadcasted_iota(jnp.int32, (WT, 128), 1) // 32
    total = None
    for h in range(4):
        pick = lane_head == h
        qh = jnp.where(pick, q, jnp.zeros_like(q))
        vh = jnp.where(pick, v, jnp.zeros_like(v))
        s = dot_nt(qh, k) * scale + (bias_of(h) + extra)
        top = jnp.max(s, axis=-1, keepdims=True)
        p = jnp.exp(s - top)
        inv = 1.0 / jnp.sum(p, axis=-1, keepdims=True)
        o = dot_nn(p.astype(BF), vh) * inv
        total = o if total is None else total + o
    store(total)


def region_mask(thr):
    def reg(dim):
        t = lax.broadcasted_iota(jnp.int32, (WT, WT), dim)
        return jnp.where(t >= 72, t - 72, t) >= thr

    return jnp.where(reg(0) == reg(1), 0.0, NEG).astype(F32)


def fine_attn_kernel(sc_ref, own_ref, lon_ref, lat_ref, gain_ref, w_ref, bias_ref, out_ref, ext, xw, q_s, k_s, v_s, mask_s, o_s):
    s0 = sc_ref[0]
    s1 = sc_ref[1]
    for l in range(4):
        for r in range(12):
            ext[l, r, 0:12] = own_ref[l, r].astype(F32)
            ext[l, r, 12:23] = lon_ref[l, r].astype(F32)
        for r in range(5):
            ext[l, 12 + r, 0:23] = lat_ref[l, r].astype(F32)
    for dp in range(2):
        for lr in range(2):
            for a in range(2):
                for b in range(6):
                    row = ((dp * 2 + lr) * 12 + a * 6 + b) * 12
                    full = ext[dp * 2 + a, s0 + lr * 6 + b]
                    xw[row : row + 12] = pltpu.roll(full, 24 - s1, 0)[0:12]
    gain = gain_ref[...]

    def project(i, _):
        rows = pl.ds(i * WT, WT)
        xn = norm_rows(xw[rows], gain).astype(BF)
        q_s[rows] = dot_nn(xn, w_ref[0]).astype(BF)
        k_s[rows] = dot_nn(xn, w_ref[1]).astype(BF)
        v_s[rows] = dot_nn(xn, w_ref[2]).astype(BF)
        return 0

    lax.fori_loop(0, 4, project, 0)

    def window(i, _):
        thr = jnp.where(i % 2 == 1, sc_ref[2], 1000)
        mask_s[...] = region_mask(thr)
        rows = pl.ds(i * WT, WT)
        for j in range(4):
            cols = slice(128 * j, 128 * j + 128)

            def store(total, cols=cols):
                o_s[rows, cols] = total

            attend_group(
                q_s[rows, cols], k_s[rows, cols], v_s[rows, cols],
                lambda h, j=j: bias_ref[4 * j + h], mask_s[...], 32 ** (-0.5), store,
            )
        return 0

    lax.fori_loop(0, 4, window, 0)
    for dp in range(2):
        for lr in range(2):
            for a in range(2):
                for b in range(6):
                    row = ((dp * 2 + lr) * 12 + a * 6 + b) * 12
                    out_ref[dp * 2 + a, lr * 6 + b] = o_s[row : row + 12].astype(BF)


def fine_attention(scalars, own, lon, lat, gain, weights, bias):
    return pl.pallas_call(
        fine_attn_kernel,
        out_shape=jax.ShapeDtypeStruct((4, 12, 12, 512), BF),
        in_specs=full_spec(7, (0,)),
        out_specs=pl.BlockSpec(memory_space=pltpu.VMEM),
        scratch_shapes=[
            pltpu.VMEM((4, 17, 24, 512), F32),
            pltpu.VMEM((576, 512), F32),
            pltpu.VMEM((576, 512), BF),
            pltpu.VMEM((576, 512), BF),
            pltpu.VMEM((576, 512), BF),
            pltpu.VMEM((WT, WT), F32),
            pltpu.VMEM((576, 512), F32),
        ],
        compiler_params=pltpu.CompilerParams(vmem_limit_bytes=VLIM),
        name="fine_attention",
    )(scalars, own, lon, lat, gain, weights, bias)


def fine_post_kernel(sc_ref, own_ref, lon_ref, lat_ref, x_ref, wo_ref, g_ref, we_ref, wr_ref, mg_ref, wm_ref, fs_ref, ci_ref, ext, xf, mf, xp, mp, tiles):
    r0 = 5 - sc_ref[0]
    turn = 16 + sc_ref[1]
    for l in range(4):
        for r in range(12):
            ext[l, 5 + r, 16:28] = own_ref[l, r].astype(F32)
            ext[l, 5 + r, 5:16] = lon_ref[l, r].astype(F32)
            own_x = x_ref[l, r].astype(F32)
            for c in range(4):
                xf[c, l, r, 0:12] = own_x[:, 128 * c : 128 * c + 128]
        for r in range(5):
            ext[l, r, 5:28] = lat_ref[l, r].astype(F32)
    for l in range(4):
        for r in range(12):
            turned = pltpu.roll(ext[l, r0 + r], turn, 0)[0:16]
            for c in range(4):
                mf[c, l, r] = turned[:, 128 * c : 128 * c + 128]
    for b in range(2):
        for a in range(2):
            for p in range(4):
                for i in range(6):
                    row = (2 * b + a) * WT + p * 36 + i * 6
                    for c in range(4):
                        cs = slice(128 * c, 128 * c + 128)
                        mp[row : row + 6, cs] = mf[c, p, 2 * i + a, pl.ds(b, 6, stride=2), :]
                        xp[row : row + 6, cs] = xf[c, p, 2 * i + a, pl.ds(b, 6, stride=2), :]
    gain = g_ref[...]
    def block(i, _):
        rows = pl.ds(i * WT, WT)
        att = (xp[rows] + dot_nn(mp[rows].astype(BF), wo_ref[...])).astype(BF).astype(F32)
        xn = norm_rows(att, gain).astype(BF)
        hid = jax.nn.gelu(dot_nn(xn, we_ref[...])).astype(BF)
        fs_ref[i] = (att + dot_nn(hid, wr_ref[...])).astype(BF)
        return 0

    lax.fori_loop(0, 4, block, 0)
    parts = [fs_ref[i].astype(F32) for i in range(4)]
    mean = sum(jnp.sum(v, axis=-1, keepdims=True) for v in parts) * (1.0 / 2048)
    parts = [v - mean for v in parts]
    var = sum(jnp.sum(v * v, axis=-1, keepdims=True) for v in parts) * (1.0 / 2048)
    inv = lax.rsqrt(var + EPS)
    acc = None
    for i in range(4):
        cs = slice(512 * i, 512 * i + 512)
        t = dot_nn((parts[i] * inv * mg_ref[:, cs]).astype(BF), wm_ref[cs, :])
        acc = t if acc is None else acc + t
    rows_to_tiles(acc, tiles, 0)
    ci_ref[...] = tiles[...].reshape(4, 6, 6, 8, 128).astype(BF)


def fine_post(scalars, own, lon, lat, field, wo, gain, we, wr, mg, wm):
    return pl.pallas_call(
        fine_post_kernel,
        out_shape=(jax.ShapeDtypeStruct((4, WT, 512), BF), jax.ShapeDtypeStruct((4, 6, 6, 8, 128), BF)),
        in_specs=full_spec(11, (0,)),
        out_specs=(pl.BlockSpec(memory_space=pltpu.VMEM), pl.BlockSpec(memory_space=pltpu.VMEM)),
        scratch_shapes=[
            pltpu.VMEM((4, 17, 32, 512), F32),
            pltpu.VMEM((4, 4, 12, 16, 128), F32),
            pltpu.VMEM((4, 4, 12, 16, 128), F32),
            pltpu.VMEM((576, 512), F32),
            pltpu.VMEM((576, 512), F32),
            pltpu.VMEM((WT * 8, 128), F32),
        ],
        compiler_params=pltpu.CompilerParams(vmem_limit_bytes=VLIM),
        name="fine_post",
    )(scalars, own, lon, lat, field, wo, gain, we, wr, mg, wm)


def coarse_attn_kernel(sc_ref, own_ref, next_ref, gain_ref, g_ref, out_ref, ext, tiles, xf, xn, acc, mask_s):
    j = pl.program_id(0)

    @pl.when(j == 0)
    def _():
        s3 = sc_ref[3]
        for half in range(2):
            for a in range(2):
                ext[a, :, 6 * half : 6 * half + 6] = own_ref[half, a].astype(F32)
                ext[a, :, 12 + 6 * half : 18 + 6 * half] = next_ref[half, a].astype(F32)
        for a in range(2):
            for b in range(6):
                row = (a * 6 + b) * 96
                tiles[row : row + 96] = ext[a, b, pl.ds(s3, 12)].reshape(96, 128)
        for c, part in enumerate(tiles_to_rows(tiles, 0, WT)):
            xf[:, 128 * c : 128 * c + 128] = part
        xn[...] = norm_rows(xf[...], gain_ref[...]).astype(BF)
        acc[...] = xf[...]
        mask_s[...] = region_mask(sc_ref[4])

    def rows_of(first, count):
        return jnp.concatenate([g_ref[0, first : first + count], g_ref[1, first : first + count]], axis=0)

    x = xn[...]
    q = dot_nt(x, rows_of(0, 64)).astype(BF)
    k = dot_nt(x, rows_of(64, 64)).astype(BF)
    v = dot_nt(x, rows_of(128, 64)).astype(BF)

    def bias_of(h):
        first = (h % 2) * 512
        hi = g_ref[h // 2, 256:400, first : first + WT].astype(F32)
        return hi + g_ref[h // 2, 256:400, first + 256 : first + 256 + WT].astype(F32)

    def store(total):
        acc[...] += dot_nn(total.astype(BF), rows_of(192, 64))

    attend_group(q, k, v, bias_of, mask_s[...], 32 ** (-0.5), store)

    @pl.when(j == 7)
    def _():
        rows_to_tiles(acc[...], tiles, 0)
        out_ref[...] = tiles[...].reshape(2, 6, 12, 8, 128).astype(BF)


def coarse_attention(scalars, own, ahead, gain, packed):
    vm = lambda: pl.BlockSpec(memory_space=pltpu.VMEM)
    return pl.pallas_call(
        coarse_attn_kernel,
        grid=(8,),
        out_shape=jax.ShapeDtypeStruct((2, 6, 12, 8, 128), BF),
        in_specs=[
            pl.BlockSpec(memory_space=pltpu.SMEM), vm(), vm(), vm(),
            pl.BlockSpec((2, 400, 1024), lambda j: (j, 0, 0)),
        ],
        out_specs=vm(),
        scratch_shapes=[
            pltpu.VMEM((2, 6, 24, 8, 128), F32),
            pltpu.VMEM((WT * 8, 128), F32),
            pltpu.VMEM((WT, 1024), F32),
            pltpu.VMEM((WT, 1024), BF),
            pltpu.VMEM((WT, 1024), F32),
            pltpu.VMEM((WT, WT), F32),
        ],
        compiler_params=pltpu.CompilerParams(vmem_limit_bytes=VLIM, dimension_semantics=("arbitrary",)),
        name="coarse_attention",
    )(scalars, own, ahead, gain, packed)


def coarse_ff_kernel(own_ref, across_ref, mate_ref, gain_ref, g_ref, keep_ref, send_ref, tiles, xn, acc):
    j = pl.program_id(0)

    @pl.when(j == 0)
    def _():
        sources = (own_ref[...], across_ref[...], mate_ref[0], mate_ref[1])
        for i, block in enumerate(sources):
            tiles[...] = block.astype(F32).reshape(WT * 8, 128)
            x = jnp.concatenate(tiles_to_rows(tiles, 0, WT), axis=1)
            xn[WT * i : WT * i + WT] = norm_rows(x, gain_ref[...]).astype(BF)
        acc[...] = jnp.zeros_like(acc)

    hid = jax.nn.gelu(dot_nt(xn[...], g_ref[0, 0:256])).astype(BF)
    acc[...] += dot_nn(hid, g_ref[0, 256:512])

    @pl.when(j == 3)
    def _():
        keep_ref[...] = acc[0 : 2 * WT]
        send_ref[...] = acc[2 * WT : 4 * WT].astype(BF)


def coarse_ff(own, across, mate, gain, packed):
    vm = lambda: pl.BlockSpec(memory_space=pltpu.VMEM)
    return pl.pallas_call(
        coarse_ff_kernel,
        grid=(4,),
        out_shape=(jax.ShapeDtypeStruct((2 * WT, 1024), F32), jax.ShapeDtypeStruct((2 * WT, 1024), BF)),
        in_specs=[vm(), vm(), vm(), vm(), pl.BlockSpec((1, 512, 1024), lambda j: (j, 0, 0))],
        out_specs=(vm(), vm()),
        scratch_shapes=[
            pltpu.VMEM((WT * 8, 128), F32),
            pltpu.VMEM((4 * WT, 1024), BF),
            pltpu.VMEM((4 * WT, 1024), F32),
        ],
        compiler_params=pltpu.CompilerParams(vmem_limit_bytes=VLIM, dimension_semantics=("arbitrary",)),
        name="coarse_ff",
    )(own, across, mate, gain, packed)


def blend_kernel(mid_ref, keep_ref, mate_ref, across_ref, wu_ref, fs_ref, out_ref, cs_ref, tiles, rows_s, grid_s):
    tiles[...] = mid_ref[...].astype(F32).reshape(WT * 8, 128)
    mid = jnp.concatenate(tiles_to_rows(tiles, 0, WT), axis=1)
    added = keep_ref[0:WT] + mate_ref[0:WT].astype(F32) + across_ref[...].astype(F32)
    rows_s[...] = mid + added
    state = rows_s[...].astype(BF)
    for p in range(4):
        for i in range(6):
            row = p * 36 + i * 6
            cs_ref[p, i] = rows_s[row : row + 6].astype(BF)
    for blk in range(4):
        b, a = blk // 2, blk % 2
        e = dot_nn(state, wu_ref[:, 512 * blk : 512 * blk + 512])
        t = fs_ref[blk].astype(F32) + e
        for p in range(4):
            for i in range(6):
                row = p * 36 + i * 6
                for c in range(4):
                    cs = slice(128 * c, 128 * c + 128)
                    grid_s[c, p, 2 * i + a, pl.ds(b, 6, stride=2), :] = t[row : row + 6, cs]
    for p in range(4):
        for r in range(12):
            for c in range(4):
                out_ref[p, r, :, 128 * c : 128 * c + 128] = grid_s[c, p, r, 0:12].astype(BF)


def blend(mid, keep, mate, across, wu, fs):
    return pl.pallas_call(
        blend_kernel,
        out_shape=(jax.ShapeDtypeStruct((4, 12, 12, 512), BF), jax.ShapeDtypeStruct((4, 6, 6, 1024), BF)),
        in_specs=full_spec(6),
        out_specs=(pl.BlockSpec(memory_space=pltpu.VMEM), pl.BlockSpec(memory_space=pltpu.VMEM)),
        scratch_shapes=[
            pltpu.VMEM((WT * 8, 128), F32),
            pltpu.VMEM((WT, 1024), F32),
            pltpu.VMEM((4, 4, 12, 16, 128), F32),
        ],
        compiler_params=pltpu.CompilerParams(vmem_limit_bytes=VLIM),
        name="blend",
    )(mid, keep, mate, across, wu, fs)


WL = 6
WW = 12


def shifted(block, axis, distance):
    devices = range(lax.axis_size(axis))
    route = [((i - distance) % len(devices), i) for i in devices]
    return lax.ppermute(block, axis, route)


def swapped(block, bit):
    return lax.ppermute(block, "lon", [(i, i ^ bit) for i in range(lax.axis_size("lon"))])


def chip_shifted(block, distance):
    count = lax.axis_size("lon")
    return lax.ppermute(block, "lon", [((i - 2 * distance) % count, i) for i in range(count)])


def in_order(core, mine, other):
    first = jnp.where(core == 0, mine, other)
    second = jnp.where(core == 0, other, mine)
    return jnp.stack([first, second])


def pack_attention(triple, output, bias):
    wide = triple.shape[0]
    columns = triple.reshape(wide, 2, 3, 32).transpose(2, 1, 3, 0).reshape(192, wide)
    padded = jnp.pad(bias, ((0, 0), (0, 0), (0, 256 - WT)))
    high = lax.reduce_precision(padded, 8, 7)
    low = padded - high
    both = jnp.stack([high, low], axis=1).astype(BF).transpose(2, 0, 1, 3).reshape(WT, 1024)
    return jnp.concatenate([columns, output, both], axis=0)


def body(
    fine_field,
    offsets,
    fine_prenorm,
    fine_triple,
    fine_bias,
    fine_output,
    fine_midnorm,
    fine_expand,
    fine_reduce,
    merge_gain,
    merge_weight,
    coarse_prenorm,
    coarse_triple,
    coarse_bias,
    coarse_output,
    coarse_midnorm,
    coarse_expand,
    coarse_reduce,
    upsample_weight,
):
    levels, lat_rows, lon_cols, channels = fine_field.shape
    lat_count = lax.axis_size("lat")
    lat_index = lax.axis_index("lat")
    fine_lat = offsets[0]
    fine_lon = offsets[1]
    coarse_lat = offsets[2]
    coarse_lon = offsets[3]
    core = lax.axis_index("lon") % 2
    attn_pack = pack_attention(coarse_triple, coarse_output, coarse_bias)
    attn_all = lax.all_gather(attn_pack, "lon", axis=0, tiled=False)
    ff_pack = jnp.concatenate([coarse_expand.T, coarse_reduce], axis=0)
    rings = [[z * 8 + y * 2 + c for y in range(4)] for z in range(2) for c in range(2)]
    ff_all = lax.all_gather(ff_pack, "lon", axis=0, tiled=False, axis_index_groups=rings)
    lon_ahead = shifted(fine_field[:, :, : WW - 1], "lon", -1)
    lat_ahead = shifted(
        jnp.concatenate([fine_field[:, : WL - 1], lon_ahead[:, : WL - 1]], axis=2), "lat", -1
    )
    half_rows = lat_rows // 2
    half_cols = lon_cols // 2
    last_band = lat_index == lat_count - 1
    scalars = jnp.stack(
        [
            fine_lat,
            fine_lon,
            jnp.where(last_band, 12 * (WL - fine_lat), 1000),
            coarse_lon,
            jnp.where(last_band, 12 * (WL - coarse_lat), 1000),
        ]
    )
    triple_heads = fine_triple.reshape(channels, -1, 3, 32).transpose(2, 0, 1, 3)
    triple_heads = triple_heads.reshape(3, channels, channels)
    mixed_fine = fine_attention(
        scalars, fine_field, lon_ahead, lat_ahead, fine_prenorm[None], triple_heads, fine_bias
    )
    lon_behind = shifted(mixed_fine[:, :, lon_cols - WW + 1 :], "lon", 1)
    tail = lat_rows - WL + 1
    lat_behind = shifted(
        jnp.concatenate([lon_behind[:, tail:], mixed_fine[:, tail:]], axis=2), "lat", 1
    )
    fine_state, coarse_own = fine_post(
        scalars, mixed_fine, lon_behind, lat_behind, fine_field, fine_output, fine_midnorm[None],
        fine_expand, fine_reduce, merge_gain[None], merge_weight,
    )
    rows_ahead = shifted(coarse_own[:, : WL - 1], "lat", -1)
    framed = lax.dynamic_slice_in_dim(
        jnp.concatenate([coarse_own, rows_ahead], axis=1), coarse_lat, half_rows, axis=1
    )
    mine = lax.dynamic_slice_in_dim(framed, 2 * core, 2, axis=0)
    other = swapped(lax.dynamic_slice_in_dim(framed, 2 - 2 * core, 2, axis=0), 1)
    chip = in_order(core, mine, other)
    chip_ahead = chip_shifted(chip, -1)
    mid_framed = coarse_attention(scalars, chip, chip_ahead, coarse_prenorm[None], attn_all)
    cols_behind = chip_shifted(mid_framed[:, :, 1:], 1)
    spread = jnp.concatenate([cols_behind, mid_framed], axis=2)
    first = WW - 1 - coarse_lon
    mine = lax.dynamic_slice_in_dim(spread, first + half_cols * core, half_cols, axis=2)
    other = swapped(
        lax.dynamic_slice_in_dim(spread, first + half_cols * (1 - core), half_cols, axis=2), 1
    )
    levels_all = in_order(core, mine, other).reshape(levels, half_rows, half_cols, 8, 128)
    rows_behind = shifted(levels_all[:, 1:], "lat", 1)
    mid_own = lax.dynamic_slice_in_dim(
        jnp.concatenate([rows_behind, levels_all], axis=1), WL - 1 - coarse_lat, half_rows, axis=1
    )
    mid_own = mid_own.reshape(WT, 8, 128)
    across = swapped(mid_own, 8)
    mate = swapped(jnp.stack([mid_own, across]), 1)
    keep, send = coarse_ff(mid_own, across, mate, coarse_midnorm[None], ff_all)
    from_mate = swapped(send, 1)
    from_across = swapped((keep[WT:] + from_mate[WT:].astype(F32)).astype(BF), 8)
    return blend(mid_own, keep, from_mate, from_across, upsample_weight, fine_state)


def solution(mesh):
    placed = (
        P(None, "lat", "lon", None),
        P(),
        P(),
        P(),
        P(),
        P(),
        P(),
        P(),
        P(),
        P(),
        P(),
        P(),
        P(None, "lon"),
        P("lon", None, None),
        P("lon", None),
        P(),
        P(None, "lon"),
        P("lon", None),
        P(),
    )
    return jax.shard_map(
        body,
        mesh=mesh,
        in_specs=placed,
        out_specs=(P(None, "lat", "lon", None), P(None, "lat", "lon", None)),
        check_vma=False,
    )
```

```python
import jax
import jax.numpy as jnp
from jax import lax
from jax.sharding import PartitionSpec as P
from jax.experimental import pallas as pl
from jax.experimental.pallas import tpu as pltpu

BF = jnp.bfloat16
F32 = jnp.float32
EPS = 1e-05
NEG = -1e30
WT = 144
VLIM = 56 * 1024 * 1024


def full_spec(n, smem=()):
    return [
        pl.BlockSpec(memory_space=pltpu.SMEM) if i in smem else pl.BlockSpec(memory_space=pltpu.VMEM)
        for i in range(n)
    ]


def norm_rows(x, gain):
    mean = jnp.mean(x, axis=-1, keepdims=True)
    off = x - mean
    var = jnp.mean(off * off, axis=-1, keepdims=True)
    return off * lax.rsqrt(var + EPS) * gain


def dot_nt(a, b):
    return lax.dot_general(a, b, (((1,), (1,)), ((), ())), preferred_element_type=F32)


def dot_nn(a, b):
    return jnp.dot(a, b, preferred_element_type=F32)


def rows_to_tiles(rows, tiles, first):
    count = rows.shape[0]
    for c in range(8):
        tiles[pl.ds(first * 8 + c, count, stride=8), :] = rows[:, 128 * c : 128 * c + 128]


def tiles_to_rows(tiles, first, count):
    return [tiles[pl.ds(first * 8 + c, count, stride=8), :] for c in range(8)]


def attend_group(q, k, v, bias_of, extra, scale, store):
    lane_head = lax.broadcasted_iota(jnp.int32, (WT, 128), 1) // 32
    total = None
    for h in range(4):
        pick = lane_head == h
        qh = jnp.where(pick, q, jnp.zeros_like(q))
        vh = jnp.where(pick, v, jnp.zeros_like(v))
        s = dot_nt(qh, k) * scale + (bias_of(h) + extra)
        top = jnp.max(s, axis=-1, keepdims=True)
        p = jnp.exp(s - top)
        inv = 1.0 / jnp.sum(p, axis=-1, keepdims=True)
        o = dot_nn(p.astype(BF), vh) * inv
        total = o if total is None else total + o
    store(total)


def region_mask(thr):
    def reg(dim):
        t = lax.broadcasted_iota(jnp.int32, (WT, WT), dim)
        return jnp.where(t >= 72, t - 72, t) >= thr

    return jnp.where(reg(0) == reg(1), 0.0, NEG).astype(F32)


def fill_frame(sc_ref, own_ref, lon_ref, lat_ref, ext, ahead):
    lat_row = jnp.where(sc_ref[4] == ahead, 15, 0)
    after = sc_ref[5] == ahead
    for l in range(4):
        for r in range(12):
            ext[l, 3 + r, 6:18] = own_ref[l, r].astype(F32)
        for r in range(3):
            ext[l, lat_row + r, 6:18] = lat_ref[l, r, 0:12].astype(F32)

    def edge(cols):
        for l in range(4):
            for r in range(12):
                ext[l, 3 + r, cols] = lon_ref[l, r].astype(F32)
            for r in range(3):
                ext[l, lat_row + r, cols] = lat_ref[l, r, 12:18].astype(F32)

    @pl.when(after)
    def _():
        edge(slice(18, 24))

    @pl.when(jnp.logical_not(after))
    def _():
        edge(slice(0, 6))


def fine_attn_kernel(sc_ref, own_ref, lon_ref, lat_ref, gain_ref, w_ref, bias_ref, out_ref, ext, xw, q_s, k_s, v_s, mask_s, o_s):
    row0 = 3 + sc_ref[0]
    turn = 18 - sc_ref[1]
    fill_frame(sc_ref, own_ref, lon_ref, lat_ref, ext, 1)
    for dp in range(2):
        for lr in range(2):
            for a in range(2):
                for b in range(6):
                    row = ((dp * 2 + lr) * 12 + a * 6 + b) * 12
                    full = ext[dp * 2 + a, row0 + lr * 6 + b]
                    xw[row : row + 12] = pltpu.roll(full, turn, 0)[0:12]
    gain = gain_ref[...]

    def project(i, _):
        rows = pl.ds(i * WT, WT)
        xn = norm_rows(xw[rows], gain).astype(BF)
        q_s[rows] = dot_nn(xn, w_ref[0]).astype(BF)
        k_s[rows] = dot_nn(xn, w_ref[1]).astype(BF)
        v_s[rows] = dot_nn(xn, w_ref[2]).astype(BF)
        return 0

    lax.fori_loop(0, 4, project, 0)

    def window(i, _):
        thr = jnp.where(i % 2 == sc_ref[3], sc_ref[2], 1000)
        mask_s[...] = region_mask(thr)
        rows = pl.ds(i * WT, WT)
        for j in range(4):
            cols = slice(128 * j, 128 * j + 128)

            def store(total, cols=cols):
                o_s[rows, cols] = total

            attend_group(
                q_s[rows, cols], k_s[rows, cols], v_s[rows, cols],
                lambda h, j=j: bias_ref[4 * j + h], mask_s[...], 32 ** (-0.5), store,
            )
        return 0

    lax.fori_loop(0, 4, window, 0)
    for dp in range(2):
        for lr in range(2):
            for a in range(2):
                for b in range(6):
                    row = ((dp * 2 + lr) * 12 + a * 6 + b) * 12
                    out_ref[dp * 2 + a, lr * 6 + b] = o_s[row : row + 12].astype(BF)


def fine_attention(scalars, own, lon, lat, gain, weights, bias):
    return pl.pallas_call(
        fine_attn_kernel,
        out_shape=jax.ShapeDtypeStruct((4, 12, 12, 512), BF),
        in_specs=full_spec(7, (0,)),
        out_specs=pl.BlockSpec(memory_space=pltpu.VMEM),
        scratch_shapes=[
            pltpu.VMEM((4, 18, 24, 512), F32),
            pltpu.VMEM((576, 512), F32),
            pltpu.VMEM((576, 512), BF),
            pltpu.VMEM((576, 512), BF),
            pltpu.VMEM((576, 512), BF),
            pltpu.VMEM((WT, WT), F32),
            pltpu.VMEM((576, 512), F32),
        ],
        compiler_params=pltpu.CompilerParams(vmem_limit_bytes=VLIM),
        name="fine_attention",
    )(scalars, own, lon, lat, gain, weights, bias)


def fine_post_kernel(sc_ref, own_ref, lon_ref, lat_ref, x_ref, wo_ref, g_ref, we_ref, wr_ref, mg_ref, wm_ref, fs_ref, ci_ref, ext, xf, mf, xp, mp, tiles):
    r0 = 3 - sc_ref[0]
    turn = (18 + sc_ref[1]) % 24
    fill_frame(sc_ref, own_ref, lon_ref, lat_ref, ext, 0)
    for l in range(4):
        for r in range(12):
            own_x = x_ref[l, r].astype(F32)
            for c in range(4):
                xf[c, l, r, 0:12] = own_x[:, 128 * c : 128 * c + 128]
    for l in range(4):
        for r in range(12):
            turned = pltpu.roll(ext[l, r0 + r], turn, 0)[0:16]
            for c in range(4):
                mf[c, l, r] = turned[:, 128 * c : 128 * c + 128]
    for b in range(2):
        for a in range(2):
            for p in range(4):
                for i in range(6):
                    row = (2 * b + a) * WT + p * 36 + i * 6
                    for c in range(4):
                        cs = slice(128 * c, 128 * c + 128)
                        mp[row : row + 6, cs] = mf[c, p, 2 * i + a, pl.ds(b, 6, stride=2), :]
                        xp[row : row + 6, cs] = xf[c, p, 2 * i + a, pl.ds(b, 6, stride=2), :]
    gain = g_ref[...]
    def block(i, _):
        rows = pl.ds(i * WT, WT)
        att = (xp[rows] + dot_nn(mp[rows].astype(BF), wo_ref[...])).astype(BF).astype(F32)
        xn = norm_rows(att, gain).astype(BF)
        hid = jax.nn.gelu(dot_nn(xn, we_ref[...])).astype(BF)
        fs_ref[i] = (att + dot_nn(hid, wr_ref[...])).astype(BF)
        return 0

    lax.fori_loop(0, 4, block, 0)
    parts = [fs_ref[i].astype(F32) for i in range(4)]
    mean = sum(jnp.sum(v, axis=-1, keepdims=True) for v in parts) * (1.0 / 2048)
    parts = [v - mean for v in parts]
    var = sum(jnp.sum(v * v, axis=-1, keepdims=True) for v in parts) * (1.0 / 2048)
    inv = lax.rsqrt(var + EPS)
    acc = None
    for i in range(4):
        cs = slice(512 * i, 512 * i + 512)
        t = dot_nn((parts[i] * inv * mg_ref[:, cs]).astype(BF), wm_ref[cs, :])
        acc = t if acc is None else acc + t
    rows_to_tiles(acc, tiles, 0)
    ci_ref[...] = tiles[...].reshape(4, 6, 6, 8, 128).astype(BF)


def fine_post(scalars, own, lon, lat, field, wo, gain, we, wr, mg, wm):
    return pl.pallas_call(
        fine_post_kernel,
        out_shape=(jax.ShapeDtypeStruct((4, WT, 512), BF), jax.ShapeDtypeStruct((4, 6, 6, 8, 128), BF)),
        in_specs=full_spec(11, (0,)),
        out_specs=(pl.BlockSpec(memory_space=pltpu.VMEM), pl.BlockSpec(memory_space=pltpu.VMEM)),
        scratch_shapes=[
            pltpu.VMEM((4, 18, 24, 512), F32),
            pltpu.VMEM((4, 4, 12, 16, 128), F32),
            pltpu.VMEM((4, 4, 12, 16, 128), F32),
            pltpu.VMEM((576, 512), F32),
            pltpu.VMEM((576, 512), F32),
            pltpu.VMEM((WT * 8, 128), F32),
        ],
        compiler_params=pltpu.CompilerParams(vmem_limit_bytes=VLIM),
        name="fine_post",
    )(scalars, own, lon, lat, field, wo, gain, we, wr, mg, wm)


def coarse_attn_kernel(sc_ref, own_ref, next_ref, gain_ref, g_ref, out_ref, ext, tiles, xf, xn, acc, mask_s):
    j = pl.program_id(0)

    @pl.when(j == 0)
    def _():
        first = 6 + sc_ref[6]
        edge = jnp.where(sc_ref[7] == 1, 18, 0)
        for a in range(2):
            for half in range(2):
                ext[a, :, 6 + 6 * half : 12 + 6 * half] = own_ref[half, a].astype(F32)
            for b in range(6):
                ext[a, b, pl.ds(edge, 6)] = next_ref[a, b].astype(F32)
        for a in range(2):
            for b in range(6):
                row = (a * 6 + b) * 96
                tiles[row : row + 96] = ext[a, b, pl.ds(first, 12)].reshape(96, 128)
        for c, part in enumerate(tiles_to_rows(tiles, 0, WT)):
            xf[:, 128 * c : 128 * c + 128] = part
        xn[...] = norm_rows(xf[...], gain_ref[...]).astype(BF)
        acc[...] = xf[...]
        mask_s[...] = region_mask(sc_ref[8])

    def rows_of(first, count):
        return jnp.concatenate([g_ref[0, first : first + count], g_ref[1, first : first + count]], axis=0)

    x = xn[...]
    q = dot_nt(x, rows_of(0, 64)).astype(BF)
    k = dot_nt(x, rows_of(64, 64)).astype(BF)
    v = dot_nt(x, rows_of(128, 64)).astype(BF)

    def bias_of(h):
        first = (h % 2) * 512
        hi = g_ref[h // 2, 256:400, first : first + WT].astype(F32)
        return hi + g_ref[h // 2, 256:400, first + 256 : first + 256 + WT].astype(F32)

    def store(total):
        acc[...] += dot_nn(total.astype(BF), rows_of(192, 64))

    attend_group(q, k, v, bias_of, mask_s[...], 32 ** (-0.5), store)

    @pl.when(j == 7)
    def _():
        rows_to_tiles(acc[...], tiles, 0)
        out_ref[...] = tiles[...].reshape(2, 6, 12, 8, 128).astype(BF)


def coarse_attention(scalars, own, ahead, gain, packed):
    vm = lambda: pl.BlockSpec(memory_space=pltpu.VMEM)
    return pl.pallas_call(
        coarse_attn_kernel,
        grid=(8,),
        out_shape=jax.ShapeDtypeStruct((2, 6, 12, 8, 128), BF),
        in_specs=[
            pl.BlockSpec(memory_space=pltpu.SMEM), vm(), vm(), vm(),
            pl.BlockSpec((2, 400, 1024), lambda j: (j, 0, 0)),
        ],
        out_specs=vm(),
        scratch_shapes=[
            pltpu.VMEM((2, 6, 24, 8, 128), F32),
            pltpu.VMEM((WT * 8, 128), F32),
            pltpu.VMEM((WT, 1024), F32),
            pltpu.VMEM((WT, 1024), BF),
            pltpu.VMEM((WT, 1024), F32),
            pltpu.VMEM((WT, WT), F32),
        ],
        compiler_params=pltpu.CompilerParams(vmem_limit_bytes=VLIM, dimension_semantics=("arbitrary",)),
        name="coarse_attention",
    )(scalars, own, ahead, gain, packed)


def coarse_ff_kernel(own_ref, across_ref, mate_ref, gain_ref, g_ref, keep_ref, send_ref, tiles, xn, acc):
    j = pl.program_id(0)

    @pl.when(j == 0)
    def _():
        sources = (own_ref[...], across_ref[...], mate_ref[0], mate_ref[1])
        for i, block in enumerate(sources):
            tiles[...] = block.astype(F32).reshape(WT * 8, 128)
            x = jnp.concatenate(tiles_to_rows(tiles, 0, WT), axis=1)
            xn[WT * i : WT * i + WT] = norm_rows(x, gain_ref[...]).astype(BF)
        acc[...] = jnp.zeros_like(acc)

    hid = jax.nn.gelu(dot_nt(xn[...], g_ref[0, 0:256])).astype(BF)
    acc[...] += dot_nn(hid, g_ref[0, 256:512])

    @pl.when(j == 3)
    def _():
        keep_ref[...] = acc[0 : 2 * WT]
        send_ref[...] = acc[2 * WT : 4 * WT].astype(BF)


def coarse_ff(own, across, mate, gain, packed):
    vm = lambda: pl.BlockSpec(memory_space=pltpu.VMEM)
    return pl.pallas_call(
        coarse_ff_kernel,
        grid=(4,),
        out_shape=(jax.ShapeDtypeStruct((2 * WT, 1024), F32), jax.ShapeDtypeStruct((2 * WT, 1024), BF)),
        in_specs=[vm(), vm(), vm(), vm(), pl.BlockSpec((1, 512, 1024), lambda j: (j, 0, 0))],
        out_specs=(vm(), vm()),
        scratch_shapes=[
            pltpu.VMEM((WT * 8, 128), F32),
            pltpu.VMEM((4 * WT, 1024), BF),
            pltpu.VMEM((4 * WT, 1024), F32),
        ],
        compiler_params=pltpu.CompilerParams(vmem_limit_bytes=VLIM, dimension_semantics=("arbitrary",)),
        name="coarse_ff",
    )(own, across, mate, gain, packed)


def blend_kernel(mid_ref, keep_ref, mate_ref, across_ref, wu_ref, fs_ref, out_ref, cs_ref, tiles, rows_s, grid_s):
    tiles[...] = mid_ref[...].astype(F32).reshape(WT * 8, 128)
    mid = jnp.concatenate(tiles_to_rows(tiles, 0, WT), axis=1)
    added = keep_ref[0:WT] + mate_ref[0:WT].astype(F32) + across_ref[...].astype(F32)
    rows_s[...] = mid + added
    state = rows_s[...].astype(BF)
    for p in range(4):
        for i in range(6):
            row = p * 36 + i * 6
            cs_ref[p, i] = rows_s[row : row + 6].astype(BF)
    for blk in range(4):
        b, a = blk // 2, blk % 2
        e = dot_nn(state, wu_ref[:, 512 * blk : 512 * blk + 512])
        t = fs_ref[blk].astype(F32) + e
        for p in range(4):
            for i in range(6):
                row = p * 36 + i * 6
                for c in range(4):
                    cs = slice(128 * c, 128 * c + 128)
                    grid_s[c, p, 2 * i + a, pl.ds(b, 6, stride=2), :] = t[row : row + 6, cs]
    for p in range(4):
        for r in range(12):
            for c in range(4):
                out_ref[p, r, :, 128 * c : 128 * c + 128] = grid_s[c, p, r, 0:12].astype(BF)


def blend(mid, keep, mate, across, wu, fs):
    return pl.pallas_call(
        blend_kernel,
        out_shape=(jax.ShapeDtypeStruct((4, 12, 12, 512), BF), jax.ShapeDtypeStruct((4, 6, 6, 1024), BF)),
        in_specs=full_spec(6),
        out_specs=(pl.BlockSpec(memory_space=pltpu.VMEM), pl.BlockSpec(memory_space=pltpu.VMEM)),
        scratch_shapes=[
            pltpu.VMEM((WT * 8, 128), F32),
            pltpu.VMEM((WT, 1024), F32),
            pltpu.VMEM((4, 4, 12, 16, 128), F32),
        ],
        compiler_params=pltpu.CompilerParams(vmem_limit_bytes=VLIM),
        name="blend",
    )(mid, keep, mate, across, wu, fs)


WL = 6
WW = 12


def shifted(block, axis, distance):
    devices = range(lax.axis_size(axis))
    route = [((i - distance) % len(devices), i) for i in devices]
    return lax.ppermute(block, axis, route)


def swapped(block, bit):
    return lax.ppermute(block, "lon", [(i, i ^ bit) for i in range(lax.axis_size("lon"))])


def chip_shifted(block, distance):
    count = lax.axis_size("lon")
    return lax.ppermute(block, "lon", [((i - 2 * distance) % count, i) for i in range(count)])


def fine_shift_lon(block, distance):
    return shifted(block, "lon", distance)


def fine_shift_lat(block, distance):
    return shifted(block, "lat", distance)


def split_shift(shift, window):
    ahead = shift <= window // 2
    return ahead, jnp.where(ahead, shift, shift - window)


def one_way(ahead, block, dim, width, move, to_frame):
    low = lambda v: lax.slice_in_dim(v, 0, width, axis=dim)
    high = lambda v: lax.slice_in_dim(v, v.shape[dim] - width, v.shape[dim], axis=dim)
    if to_frame:
        return lax.cond(ahead, lambda v: move(low(v), -1), lambda v: move(high(v), 1), block)
    return lax.cond(ahead, lambda v: move(high(v), 1), lambda v: move(low(v), -1), block)


def edge_rows(ahead, block, piece, to_frame):
    low = lambda v: jnp.concatenate([v[0][:, :3], v[1][:, :3]], axis=2)
    high = lambda v: jnp.concatenate([v[0][:, -3:], v[1][:, -3:]], axis=2)
    pair = (block, piece)
    if to_frame:
        return lax.cond(
            ahead, lambda v: fine_shift_lat(low(v), -1), lambda v: fine_shift_lat(high(v), 1), pair
        )
    return lax.cond(
        ahead, lambda v: fine_shift_lat(high(v), 1), lambda v: fine_shift_lat(low(v), -1), pair
    )


def in_order(core, mine, other):
    first = jnp.where(core == 0, mine, other)
    second = jnp.where(core == 0, other, mine)
    return jnp.stack([first, second])


def pack_attention(triple, output, bias):
    wide = triple.shape[0]
    columns = triple.reshape(wide, 2, 3, 32).transpose(2, 1, 3, 0).reshape(192, wide)
    padded = jnp.pad(bias, ((0, 0), (0, 0), (0, 256 - WT)))
    high = lax.reduce_precision(padded, 8, 7)
    low = padded - high
    both = jnp.stack([high, low], axis=1).astype(BF).transpose(2, 0, 1, 3).reshape(WT, 1024)
    return jnp.concatenate([columns, output, both], axis=0)


def body(
    fine_field,
    offsets,
    fine_prenorm,
    fine_triple,
    fine_bias,
    fine_output,
    fine_midnorm,
    fine_expand,
    fine_reduce,
    merge_gain,
    merge_weight,
    coarse_prenorm,
    coarse_triple,
    coarse_bias,
    coarse_output,
    coarse_midnorm,
    coarse_expand,
    coarse_reduce,
    upsample_weight,
):
    levels, lat_rows, lon_cols, channels = fine_field.shape
    lat_count = lax.axis_size("lat")
    lat_index = lax.axis_index("lat")
    fine_lat = offsets[0]
    fine_lon = offsets[1]
    coarse_lat = offsets[2]
    coarse_lon = offsets[3]
    core = lax.axis_index("lon") % 2
    attn_pack = pack_attention(coarse_triple, coarse_output, coarse_bias)
    attn_all = lax.all_gather(attn_pack, "lon", axis=0, tiled=False)
    ff_pack = jnp.concatenate([coarse_expand.T, coarse_reduce], axis=0)
    rings = [[z * 8 + y * 2 + c for y in range(4)] for z in range(2) for c in range(2)]
    ff_all = lax.all_gather(ff_pack, "lon", axis=0, tiled=False, axis_index_groups=rings)
    fine_up, fine_row = split_shift(fine_lat, WL)
    fine_right, fine_col = split_shift(fine_lon, WW)
    coarse_up, coarse_row = split_shift(coarse_lat, WL)
    coarse_right, coarse_col = split_shift(coarse_lon, WW)
    lon_piece = one_way(fine_right, fine_field, 2, 6, fine_shift_lon, True)
    lat_piece = edge_rows(fine_up, fine_field, lon_piece, True)
    half_rows = lat_rows // 2
    half_cols = lon_cols // 2


    def threshold(up, shift):
        band = jnp.where(up, lat_count - 1, 0)
        return jnp.where(lat_index == band, 12 * (WL - shift), 1000)

    scalars = jnp.stack(
        [
            fine_row,
            fine_col,
            threshold(fine_up, fine_lat),
            fine_up.astype(jnp.int32),
            fine_up.astype(jnp.int32),
            fine_right.astype(jnp.int32),
            coarse_col,
            coarse_right.astype(jnp.int32),
            threshold(coarse_up, coarse_lat),
        ]
    )
    triple_heads = fine_triple.reshape(channels, -1, 3, 32).transpose(2, 0, 1, 3)
    triple_heads = triple_heads.reshape(3, channels, channels)
    mixed_fine = fine_attention(
        scalars, fine_field, lon_piece, lat_piece, fine_prenorm[None], triple_heads, fine_bias
    )
    lon_piece = one_way(fine_right, mixed_fine, 2, 6, fine_shift_lon, False)
    lat_piece = edge_rows(fine_up, mixed_fine, lon_piece, False)
    fine_state, coarse_own = fine_post(
        scalars, mixed_fine, lon_piece, lat_piece, fine_field, fine_output, fine_midnorm[None],
        fine_expand, fine_reduce, merge_gain[None], merge_weight,
    )
    rows_piece = one_way(coarse_up, coarse_own, 1, 3, fine_shift_lat, True)
    framed = lax.dynamic_slice_in_dim(
        jnp.concatenate([rows_piece, coarse_own, rows_piece], axis=1), 3 + coarse_row, half_rows, axis=1
    )
    mine = lax.dynamic_slice_in_dim(framed, 2 * core, 2, axis=0)
    other = swapped(lax.dynamic_slice_in_dim(framed, 2 - 2 * core, 2, axis=0), 1)
    chip = in_order(core, mine, other)
    chip_piece = lax.cond(
        coarse_right, lambda v: chip_shifted(v[0], -1), lambda v: chip_shifted(v[1], 1), chip
    )
    mid_framed = coarse_attention(scalars, chip, chip_piece, coarse_prenorm[None], attn_all)
    cols_piece = one_way(coarse_right, mid_framed, 2, 6, chip_shifted, False)
    spread = jnp.concatenate([cols_piece, mid_framed, cols_piece], axis=2)
    first = 6 - coarse_col
    mine = lax.dynamic_slice_in_dim(spread, first + half_cols * core, half_cols, axis=2)
    other = swapped(
        lax.dynamic_slice_in_dim(spread, first + half_cols * (1 - core), half_cols, axis=2), 1
    )
    levels_all = in_order(core, mine, other).reshape(levels, half_rows, half_cols, 8, 128)
    rows_piece = one_way(coarse_up, levels_all, 1, 3, fine_shift_lat, False)
    mid_own = lax.dynamic_slice_in_dim(
        jnp.concatenate([rows_piece, levels_all, rows_piece], axis=1), 3 - coarse_row, half_rows, axis=1
    )
    mid_own = mid_own.reshape(WT, 8, 128)
    across = swapped(mid_own, 8)
    mate = swapped(jnp.stack([mid_own, across]), 1)
    keep, send = coarse_ff(mid_own, across, mate, coarse_midnorm[None], ff_all)
    from_mate = swapped(send, 1)
    from_across = swapped((keep[WT:] + from_mate[WT:].astype(F32)).astype(BF), 8)
    return blend(mid_own, keep, from_mate, from_across, upsample_weight, fine_state)


def solution(mesh):
    placed = (
        P(None, "lat", "lon", None),
        P(),
        P(),
        P(),
        P(),
        P(),
        P(),
        P(),
        P(),
        P(),
        P(),
        P(),
        P(None, "lon"),
        P("lon", None, None),
        P("lon", None),
        P(),
        P(None, "lon"),
        P("lon", None),
        P(),
    )
    return jax.shard_map(
        body,
        mesh=mesh,
        in_specs=placed,
        out_specs=(P(None, "lat", "lon", None), P(None, "lat", "lon", None)),
        check_vma=False,
    )
```

```python
import jax
import jax.numpy as jnp
from jax import lax
from jax.sharding import PartitionSpec as P
from jax.experimental import pallas as pl
from jax.experimental.pallas import tpu as pltpu

BF = jnp.bfloat16
F32 = jnp.float32
EPS = 1e-05
NEG = -1e30
WT = 144
VLIM = 56 * 1024 * 1024


def full_spec(n, smem=()):
    return [
        pl.BlockSpec(memory_space=pltpu.SMEM) if i in smem else pl.BlockSpec(memory_space=pltpu.VMEM)
        for i in range(n)
    ]


def norm_rows(x, gain):
    mean = jnp.mean(x, axis=-1, keepdims=True)
    off = x - mean
    var = jnp.mean(off * off, axis=-1, keepdims=True)
    return off * lax.rsqrt(var + EPS) * gain


def dot_nt(a, b):
    return lax.dot_general(a, b, (((1,), (1,)), ((), ())), preferred_element_type=F32)


def dot_nn(a, b):
    return jnp.dot(a, b, preferred_element_type=F32)


def rows_to_tiles(rows, tiles, first):
    count = rows.shape[0]
    for c in range(8):
        tiles[pl.ds(first * 8 + c, count, stride=8), :] = rows[:, 128 * c : 128 * c + 128]


def tiles_to_rows(tiles, first, count):
    return [tiles[pl.ds(first * 8 + c, count, stride=8), :] for c in range(8)]


def attend_group(q, k, v, bias_of, extra, scale, store):
    lane_head = lax.broadcasted_iota(jnp.int32, (WT, 128), 1) // 32
    total = None
    for h in range(4):
        pick = lane_head == h
        qh = jnp.where(pick, q, jnp.zeros_like(q))
        vh = jnp.where(pick, v, jnp.zeros_like(v))
        s = dot_nt(qh, k) * scale + (bias_of(h) + extra)
        top = jnp.max(s, axis=-1, keepdims=True)
        p = jnp.exp(s - top)
        inv = 1.0 / jnp.sum(p, axis=-1, keepdims=True)
        o = dot_nn(p.astype(BF), vh) * inv
        total = o if total is None else total + o
    store(total)


def region_mask(thr):
    def reg(dim):
        t = lax.broadcasted_iota(jnp.int32, (WT, WT), dim)
        return jnp.where(t >= 72, t - 72, t) >= thr

    return jnp.where(reg(0) == reg(1), 0.0, NEG).astype(F32)


def fill_frame(sc_ref, own_ref, lon_ref, lat_ref, ext, ahead):
    lat_row = jnp.where(sc_ref[4] == ahead, 15, 0)
    after = sc_ref[5] == ahead
    for l in range(4):
        for r in range(12):
            ext[l, 3 + r, 6:18] = own_ref[l, r].astype(F32)
        for r in range(3):
            ext[l, lat_row + r, 6:18] = lat_ref[l, r, 0:12].astype(F32)

    def edge(cols):
        for l in range(4):
            for r in range(12):
                ext[l, 3 + r, cols] = lon_ref[l, r].astype(F32)
            for r in range(3):
                ext[l, lat_row + r, cols] = lat_ref[l, r, 12:18].astype(F32)

    @pl.when(after)
    def _():
        edge(slice(18, 24))

    @pl.when(jnp.logical_not(after))
    def _():
        edge(slice(0, 6))


def fine_attn_kernel(sc_ref, own_ref, lon_ref, lat_ref, gain_ref, w_ref, bias_ref, out_ref, ext, xw, xn, q_s, k_s, v_s, mask_s, o_s):
    row0 = 3 + sc_ref[0]
    turn = 18 - sc_ref[1]
    fill_frame(sc_ref, own_ref, lon_ref, lat_ref, ext, 1)
    for dp in range(2):
        for lr in range(2):
            for a in range(2):
                for b in range(6):
                    row = ((dp * 2 + lr) * 12 + a * 6 + b) * 12
                    full = ext[dp * 2 + a, row0 + lr * 6 + b]
                    xw[row : row + 12] = pltpu.roll(full, turn, 0)[0:12]
    gain = gain_ref[...]
    for i in range(4):
        xn[WT * i : WT * i + WT] = norm_rows(xw[WT * i : WT * i + WT], gain).astype(BF)
    place = lax.broadcasted_iota(jnp.int32, (384, 384), 1)
    source = ((place >> 5) & 3) * 96 + (place >> 7) * 32 + (place & 31)
    order = (lax.broadcasted_iota(jnp.int32, (384, 384), 0) == source).astype(F32).astype(BF)
    for j in range(4):
        cols = slice(128 * j, 128 * j + 128)
        w = dot_nn(w_ref[:, 384 * j : 384 * j + 384], order).astype(BF)
        y = dot_nn(xn[...], w).astype(BF)
        q_s[:, cols] = y[:, 0:128]
        k_s[:, cols] = y[:, 128:256]
        v_s[:, cols] = y[:, 256:384]

    def window(i, _):
        thr = jnp.where(i % 2 == sc_ref[3], sc_ref[2], 1000)
        mask_s[...] = region_mask(thr)
        rows = pl.ds(i * WT, WT)
        for j in range(4):
            cols = slice(128 * j, 128 * j + 128)

            def store(total, cols=cols):
                o_s[rows, cols] = total

            attend_group(
                q_s[rows, cols], k_s[rows, cols], v_s[rows, cols],
                lambda h, j=j: bias_ref[4 * j + h], mask_s[...], 32 ** (-0.5), store,
            )
        return 0

    lax.fori_loop(0, 4, window, 0)
    for dp in range(2):
        for lr in range(2):
            for a in range(2):
                for b in range(6):
                    row = ((dp * 2 + lr) * 12 + a * 6 + b) * 12
                    out_ref[dp * 2 + a, lr * 6 + b] = o_s[row : row + 12].astype(BF)


def fine_attention(scalars, own, lon, lat, gain, weights, bias):
    return pl.pallas_call(
        fine_attn_kernel,
        out_shape=jax.ShapeDtypeStruct((4, 12, 12, 512), BF),
        in_specs=full_spec(7, (0,)),
        out_specs=pl.BlockSpec(memory_space=pltpu.VMEM),
        scratch_shapes=[
            pltpu.VMEM((4, 18, 24, 512), F32),
            pltpu.VMEM((576, 512), F32),
            pltpu.VMEM((576, 512), BF),
            pltpu.VMEM((576, 512), BF),
            pltpu.VMEM((576, 512), BF),
            pltpu.VMEM((576, 512), BF),
            pltpu.VMEM((WT, WT), F32),
            pltpu.VMEM((576, 512), F32),
        ],
        compiler_params=pltpu.CompilerParams(vmem_limit_bytes=VLIM),
        name="fine_attention",
    )(scalars, own, lon, lat, gain, weights, bias)


def fine_post_kernel(sc_ref, own_ref, lon_ref, lat_ref, x_ref, wo_ref, g_ref, we_ref, wr_ref, mg_ref, wm_ref, fs_ref, ci_ref, ext, xf, mf, xp, mp, tiles):
    r0 = 3 - sc_ref[0]
    turn = (18 + sc_ref[1]) % 24
    fill_frame(sc_ref, own_ref, lon_ref, lat_ref, ext, 0)
    for l in range(4):
        for r in range(12):
            own_x = x_ref[l, r].astype(F32)
            for c in range(4):
                xf[c, l, r, 0:12] = own_x[:, 128 * c : 128 * c + 128]
    for l in range(4):
        for r in range(12):
            turned = pltpu.roll(ext[l, r0 + r], turn, 0)[0:16]
            for c in range(4):
                mf[c, l, r] = turned[:, 128 * c : 128 * c + 128]
    for b in range(2):
        for a in range(2):
            for p in range(4):
                for i in range(6):
                    row = (2 * b + a) * WT + p * 36 + i * 6
                    for c in range(4):
                        cs = slice(128 * c, 128 * c + 128)
                        mp[row : row + 6, cs] = mf[c, p, 2 * i + a, pl.ds(b, 6, stride=2), :]
                        xp[row : row + 6, cs] = xf[c, p, 2 * i + a, pl.ds(b, 6, stride=2), :]
    gain = g_ref[...]
    def block(i, _):
        rows = pl.ds(i * WT, WT)
        att = (xp[rows] + dot_nn(mp[rows].astype(BF), wo_ref[...])).astype(BF).astype(F32)
        xn = norm_rows(att, gain).astype(BF)
        hid = jax.nn.gelu(dot_nn(xn, we_ref[...])).astype(BF)
        fs_ref[i] = (att + dot_nn(hid, wr_ref[...])).astype(BF)
        return 0

    lax.fori_loop(0, 4, block, 0)
    parts = [fs_ref[i].astype(F32) for i in range(4)]
    mean = sum(jnp.sum(v, axis=-1, keepdims=True) for v in parts) * (1.0 / 2048)
    parts = [v - mean for v in parts]
    var = sum(jnp.sum(v * v, axis=-1, keepdims=True) for v in parts) * (1.0 / 2048)
    inv = lax.rsqrt(var + EPS)
    acc = None
    for i in range(4):
        cs = slice(512 * i, 512 * i + 512)
        t = dot_nn((parts[i] * inv * mg_ref[:, cs]).astype(BF), wm_ref[cs, :])
        acc = t if acc is None else acc + t
    rows_to_tiles(acc, tiles, 0)
    ci_ref[...] = tiles[...].reshape(4, 6, 6, 8, 128).astype(BF)


def fine_post(scalars, own, lon, lat, field, wo, gain, we, wr, mg, wm):
    return pl.pallas_call(
        fine_post_kernel,
        out_shape=(jax.ShapeDtypeStruct((4, WT, 512), BF), jax.ShapeDtypeStruct((4, 6, 6, 8, 128), BF)),
        in_specs=full_spec(11, (0,)),
        out_specs=(pl.BlockSpec(memory_space=pltpu.VMEM), pl.BlockSpec(memory_space=pltpu.VMEM)),
        scratch_shapes=[
            pltpu.VMEM((4, 18, 24, 512), F32),
            pltpu.VMEM((4, 4, 12, 16, 128), F32),
            pltpu.VMEM((4, 4, 12, 16, 128), F32),
            pltpu.VMEM((576, 512), F32),
            pltpu.VMEM((576, 512), F32),
            pltpu.VMEM((WT * 8, 128), F32),
        ],
        compiler_params=pltpu.CompilerParams(vmem_limit_bytes=VLIM),
        name="fine_post",
    )(scalars, own, lon, lat, field, wo, gain, we, wr, mg, wm)


def coarse_attn_kernel(sc_ref, own_ref, next_ref, gain_ref, g_ref, out_ref, ext, tiles, xf, xn, acc, mask_s):
    j = pl.program_id(0)

    @pl.when(j == 0)
    def _():
        first = 6 + sc_ref[6]
        edge = jnp.where(sc_ref[7] == 1, 18, 0)
        for a in range(2):
            for half in range(2):
                ext[a, :, 6 + 6 * half : 12 + 6 * half] = own_ref[half, a].astype(F32)
            for b in range(6):
                ext[a, b, pl.ds(edge, 6)] = next_ref[a, b].astype(F32)
        for a in range(2):
            for b in range(6):
                row = (a * 6 + b) * 96
                tiles[row : row + 96] = ext[a, b, pl.ds(first, 12)].reshape(96, 128)
        for c, part in enumerate(tiles_to_rows(tiles, 0, WT)):
            xf[:, 128 * c : 128 * c + 128] = part
        xn[...] = norm_rows(xf[...], gain_ref[...]).astype(BF)
        acc[...] = xf[...]
        mask_s[...] = region_mask(sc_ref[8])

    def rows_of(first, count):
        return jnp.concatenate([g_ref[0, first : first + count], g_ref[1, first : first + count]], axis=0)

    x = xn[...]
    q = dot_nt(x, rows_of(0, 64)).astype(BF)
    k = dot_nt(x, rows_of(64, 64)).astype(BF)
    v = dot_nt(x, rows_of(128, 64)).astype(BF)

    def bias_of(h):
        first = (h % 2) * 512
        hi = g_ref[h // 2, 256:400, first : first + WT].astype(F32)
        return hi + g_ref[h // 2, 256:400, first + 256 : first + 256 + WT].astype(F32)

    def store(total):
        acc[...] += dot_nn(total.astype(BF), rows_of(192, 64))

    attend_group(q, k, v, bias_of, mask_s[...], 32 ** (-0.5), store)

    @pl.when(j == 7)
    def _():
        rows_to_tiles(acc[...], tiles, 0)
        out_ref[...] = tiles[...].reshape(2, 6, 12, 8, 128).astype(BF)


def coarse_attention(scalars, own, ahead, gain, packed):
    vm = lambda: pl.BlockSpec(memory_space=pltpu.VMEM)
    return pl.pallas_call(
        coarse_attn_kernel,
        grid=(8,),
        out_shape=jax.ShapeDtypeStruct((2, 6, 12, 8, 128), BF),
        in_specs=[
            pl.BlockSpec(memory_space=pltpu.SMEM), vm(), vm(), vm(),
            pl.BlockSpec((2, 400, 1024), lambda j: (j, 0, 0)),
        ],
        out_specs=vm(),
        scratch_shapes=[
            pltpu.VMEM((2, 6, 24, 8, 128), F32),
            pltpu.VMEM((WT * 8, 128), F32),
            pltpu.VMEM((WT, 1024), F32),
            pltpu.VMEM((WT, 1024), BF),
            pltpu.VMEM((WT, 1024), F32),
            pltpu.VMEM((WT, WT), F32),
        ],
        compiler_params=pltpu.CompilerParams(vmem_limit_bytes=VLIM, dimension_semantics=("arbitrary",)),
        name="coarse_attention",
    )(scalars, own, ahead, gain, packed)


def coarse_ff_kernel(own_ref, across_ref, mate_ref, gain_ref, g_ref, keep_ref, send_ref, tiles, xn, acc):
    sources = (own_ref[...], across_ref[...], mate_ref[0], mate_ref[1])
    for i, block in enumerate(sources):
        tiles[...] = block.astype(F32).reshape(WT * 8, 128)
        x = jnp.concatenate(tiles_to_rows(tiles, 0, WT), axis=1)
        xn[WT * i : WT * i + WT] = norm_rows(x, gain_ref[...]).astype(BF)
    for half in (1, 0):
        rows = slice(2 * WT * half, 2 * WT * half + 2 * WT)
        for i in range(4):
            hid = jax.nn.gelu(dot_nt(xn[rows], g_ref[i, 0:256])).astype(BF)
            part = dot_nn(hid, g_ref[i, 256:512])
            if i == 0:
                acc[...] = part
            else:
                acc[...] += part
        if half:
            send_ref[...] = acc[...].astype(BF)
        else:
            keep_ref[...] = acc[...]


def coarse_ff(own, across, mate, gain, packed):
    vm = lambda: pl.BlockSpec(memory_space=pltpu.VMEM)
    return pl.pallas_call(
        coarse_ff_kernel,
        out_shape=(jax.ShapeDtypeStruct((2 * WT, 1024), F32), jax.ShapeDtypeStruct((2 * WT, 1024), BF)),
        in_specs=full_spec(5),
        out_specs=(vm(), vm()),
        scratch_shapes=[
            pltpu.VMEM((WT * 8, 128), F32),
            pltpu.VMEM((4 * WT, 1024), BF),
            pltpu.VMEM((2 * WT, 1024), F32),
        ],
        compiler_params=pltpu.CompilerParams(vmem_limit_bytes=VLIM),
        name="coarse_ff",
    )(own, across, mate, gain, packed)


def blend_kernel(mid_ref, keep_ref, mate_ref, across_ref, wu_ref, fs_ref, out_ref, cs_ref, tiles, rows_s, grid_s):
    tiles[...] = mid_ref[...].astype(F32).reshape(WT * 8, 128)
    mid = jnp.concatenate(tiles_to_rows(tiles, 0, WT), axis=1)
    added = keep_ref[0:WT] + mate_ref[0:WT].astype(F32) + across_ref[...].astype(F32)
    rows_s[...] = mid + added
    state = rows_s[...].astype(BF)
    for p in range(4):
        for i in range(6):
            row = p * 36 + i * 6
            cs_ref[p, i] = rows_s[row : row + 6].astype(BF)
    for blk in range(4):
        b, a = blk // 2, blk % 2
        e = dot_nn(state, wu_ref[:, 512 * blk : 512 * blk + 512])
        t = fs_ref[blk].astype(F32) + e
        for p in range(4):
            for i in range(6):
                row = p * 36 + i * 6
                for c in range(4):
                    cs = slice(128 * c, 128 * c + 128)
                    grid_s[c, p, 2 * i + a, pl.ds(b, 6, stride=2), :] = t[row : row + 6, cs]
    for p in range(4):
        for r in range(12):
            for c in range(4):
                out_ref[p, r, :, 128 * c : 128 * c + 128] = grid_s[c, p, r, 0:12].astype(BF)


def blend(mid, keep, mate, across, wu, fs):
    return pl.pallas_call(
        blend_kernel,
        out_shape=(jax.ShapeDtypeStruct((4, 12, 12, 512), BF), jax.ShapeDtypeStruct((4, 6, 6, 1024), BF)),
        in_specs=full_spec(6),
        out_specs=(pl.BlockSpec(memory_space=pltpu.VMEM), pl.BlockSpec(memory_space=pltpu.VMEM)),
        scratch_shapes=[
            pltpu.VMEM((WT * 8, 128), F32),
            pltpu.VMEM((WT, 1024), F32),
            pltpu.VMEM((4, 4, 12, 16, 128), F32),
        ],
        compiler_params=pltpu.CompilerParams(vmem_limit_bytes=VLIM),
        name="blend",
    )(mid, keep, mate, across, wu, fs)


WL = 6
WW = 12


def shifted(block, axis, distance):
    devices = range(lax.axis_size(axis))
    route = [((i - distance) % len(devices), i) for i in devices]
    return lax.ppermute(block, axis, route)


def swapped(block, bit):
    return lax.ppermute(block, "lon", [(i, i ^ bit) for i in range(lax.axis_size("lon"))])


def chip_shifted(block, distance):
    count = lax.axis_size("lon")
    return lax.ppermute(block, "lon", [((i - 2 * distance) % count, i) for i in range(count)])


def fine_shift_lon(block, distance):
    return shifted(block, "lon", distance)


def fine_shift_lat(block, distance):
    return shifted(block, "lat", distance)


def split_shift(shift, window):
    ahead = shift <= window // 2
    return ahead, jnp.where(ahead, shift, shift - window)


LAT_PLAN = ((1, 1), (1, 2), (1, 3), (-1, 2), (-1, 1))
LON_PLAN = ((1, 1), (1, 3), (1, 6), (-1, 6), (-1, 3), (-1, 1))


def halo(choice, plan, low, high, dim, full, move, to_frame):
    def branch(side, width):
        def send(edges):
            if side == (1 if to_frame else -1):
                piece = move(lax.slice_in_dim(edges[0], 0, width, axis=dim), -1)
                room = (0, full - width)
            else:
                size = edges[1].shape[dim]
                piece = move(lax.slice_in_dim(edges[1], size - width, size, axis=dim), 1)
                room = (full - width, 0)
            return jnp.pad(piece, [room if i == dim else (0, 0) for i in range(piece.ndim)])

        return send

    return lax.switch(choice, [branch(*entry) for entry in plan], (low, high))


def fine_rows(choice, low, high, piece, to_frame):
    def move(edges, distance):
        return fine_shift_lat(jnp.concatenate(edges, axis=2), distance)

    def branch(side, width):
        def send(pair):
            if side == (1 if to_frame else -1):
                return jnp.pad(move([pair[0][:, :width], pair[2][:, :width]], -1), ((0, 0), (0, 3 - width), (0, 0), (0, 0)))
            return jnp.pad(move([pair[1][:, -width:], pair[2][:, -width:]], 1), ((0, 0), (3 - width, 0), (0, 0), (0, 0)))

        return send

    return lax.switch(choice, [branch(*entry) for entry in LAT_PLAN], (low, high, piece))


def plan_choice(shift, steps):
    return sum((shift >= step).astype(jnp.int32) for step in steps)


def in_order(core, mine, other):
    first = jnp.where(core == 0, mine, other)
    second = jnp.where(core == 0, other, mine)
    return jnp.stack([first, second])


def pack_attention(triple, output, bias):
    wide = triple.shape[0]
    columns = triple.reshape(wide, 2, 3, 32).transpose(2, 1, 3, 0).reshape(192, wide)
    padded = jnp.pad(bias, ((0, 0), (0, 0), (0, 256 - WT)))
    high = lax.reduce_precision(padded, 8, 7)
    low = padded - high
    both = jnp.stack([high, low], axis=1).astype(BF).transpose(2, 0, 1, 3).reshape(WT, 1024)
    return jnp.concatenate([columns, output, both], axis=0)


def body(
    fine_field,
    offsets,
    fine_prenorm,
    fine_triple,
    fine_bias,
    fine_output,
    fine_midnorm,
    fine_expand,
    fine_reduce,
    merge_gain,
    merge_weight,
    coarse_prenorm,
    coarse_triple,
    coarse_bias,
    coarse_output,
    coarse_midnorm,
    coarse_expand,
    coarse_reduce,
    upsample_weight,
):
    levels, lat_rows, lon_cols, channels = fine_field.shape
    lat_count = lax.axis_size("lat")
    lat_index = lax.axis_index("lat")
    fine_lat = offsets[0]
    fine_lon = offsets[1]
    coarse_lat = offsets[2]
    coarse_lon = offsets[3]
    core = lax.axis_index("lon") % 2
    fine_up, fine_row = split_shift(fine_lat, WL)
    fine_right, fine_col = split_shift(fine_lon, WW)
    coarse_up, coarse_row = split_shift(coarse_lat, WL)
    coarse_right, coarse_col = split_shift(coarse_lon, WW)
    fine_lat_plan = plan_choice(fine_lat, (2, 3, 4, 5))
    fine_lon_plan = plan_choice(fine_lon, (2, 4, 7, 9, 11))
    coarse_lat_plan = plan_choice(coarse_lat, (2, 3, 4, 5))
    coarse_lon_plan = plan_choice(coarse_lon, (2, 4, 7, 9, 11))
    lon_piece = halo(
        fine_lon_plan, LON_PLAN, fine_field[:, :, :6], fine_field[:, :, -6:], 2, 6, fine_shift_lon, True
    )
    attn_pack = pack_attention(coarse_triple, coarse_output, coarse_bias)
    lon_piece, attn_pack, low_rows, high_rows = lax.optimization_barrier(
        (lon_piece, attn_pack, fine_field[:, :3], fine_field[:, -3:])
    )
    attn_all = lax.all_gather(attn_pack, "lon", axis=0, tiled=False)
    ff_pack = jnp.concatenate([coarse_expand.T, coarse_reduce], axis=0)
    rings = [[z * 8 + y * 2 + c for y in range(4)] for z in range(2) for c in range(2)]
    ff_all = lax.all_gather(ff_pack, "lon", axis=0, tiled=False, axis_index_groups=rings)
    lat_piece = fine_rows(fine_lat_plan, low_rows, high_rows, lon_piece, True)
    half_rows = lat_rows // 2
    half_cols = lon_cols // 2


    def threshold(up, shift):
        band = jnp.where(up, lat_count - 1, 0)
        return jnp.where(lat_index == band, 12 * (WL - shift), 1000)

    scalars = jnp.stack(
        [
            fine_row,
            fine_col,
            threshold(fine_up, fine_lat),
            fine_up.astype(jnp.int32),
            fine_up.astype(jnp.int32),
            fine_right.astype(jnp.int32),
            coarse_col,
            coarse_right.astype(jnp.int32),
            threshold(coarse_up, coarse_lat),
        ]
    )
    mixed_fine = fine_attention(
        scalars, fine_field, lon_piece, lat_piece, fine_prenorm[None], fine_triple, fine_bias
    )
    lon_piece = halo(fine_lon_plan, LON_PLAN, mixed_fine, mixed_fine, 2, 6, fine_shift_lon, False)
    lat_piece = fine_rows(fine_lat_plan, mixed_fine, mixed_fine, lon_piece, False)
    fine_state, coarse_own = fine_post(
        scalars, mixed_fine, lon_piece, lat_piece, fine_field, fine_output, fine_midnorm[None],
        fine_expand, fine_reduce, merge_gain[None], merge_weight,
    )
    rows_piece = halo(coarse_lat_plan, LAT_PLAN, coarse_own, coarse_own, 1, 3, fine_shift_lat, True)
    framed = lax.dynamic_slice_in_dim(
        jnp.concatenate([rows_piece, coarse_own, rows_piece], axis=1), 3 + coarse_row, half_rows, axis=1
    )
    mine = lax.dynamic_slice_in_dim(framed, 2 * core, 2, axis=0)
    other = swapped(lax.dynamic_slice_in_dim(framed, 2 - 2 * core, 2, axis=0), 1)
    chip = in_order(core, mine, other)
    chip_piece = halo(coarse_lon_plan, LON_PLAN, chip[0], chip[1], 2, 6, chip_shifted, True)
    mid_framed = coarse_attention(scalars, chip, chip_piece, coarse_prenorm[None], attn_all)
    cols_piece = halo(coarse_lon_plan, LON_PLAN, mid_framed, mid_framed, 2, 6, chip_shifted, False)
    spread = jnp.concatenate([cols_piece, mid_framed, cols_piece], axis=2)
    first = 6 - coarse_col
    mine = lax.dynamic_slice_in_dim(spread, first + half_cols * core, half_cols, axis=2)
    other = swapped(
        lax.dynamic_slice_in_dim(spread, first + half_cols * (1 - core), half_cols, axis=2), 1
    )
    levels_all = in_order(core, mine, other).reshape(levels, half_rows, half_cols, 8, 128)
    rows_piece = halo(coarse_lat_plan, LAT_PLAN, levels_all, levels_all, 1, 3, fine_shift_lat, False)
    mid_own = lax.dynamic_slice_in_dim(
        jnp.concatenate([rows_piece, levels_all, rows_piece], axis=1), 3 - coarse_row, half_rows, axis=1
    )
    mid_own = mid_own.reshape(WT, 8, 128)
    across = swapped(mid_own, 8)
    mate = swapped(jnp.stack([mid_own, across]), 1)
    keep, send = coarse_ff(mid_own, across, mate, coarse_midnorm[None], ff_all)
    from_mate = swapped(send, 1)
    from_across = swapped((keep[WT:] + from_mate[WT:].astype(F32)).astype(BF), 8)
    return blend(mid_own, keep, from_mate, from_across, upsample_weight, fine_state)


def solution(mesh):
    placed = (
        P(None, "lat", "lon", None),
        P(),
        P(),
        P(),
        P(),
        P(),
        P(),
        P(),
        P(),
        P(),
        P(),
        P(),
        P(None, "lon"),
        P("lon", None, None),
        P("lon", None),
        P(),
        P(None, "lon"),
        P("lon", None),
        P(),
    )
    return jax.shard_map(
        body,
        mesh=mesh,
        in_specs=placed,
        out_specs=(P(None, "lat", "lon", None), P(None, "lat", "lon", None)),
        check_vma=False,
    )
```

```python
import jax
import jax.numpy as jnp
from jax import lax
from jax.sharding import PartitionSpec as P
from jax.experimental import pallas as pl
from jax.experimental.pallas import tpu as pltpu

BF = jnp.bfloat16
F32 = jnp.float32
EPS = 1e-05
NEG = -1e30
WT = 144
VLIM = 56 * 1024 * 1024


def full_spec(n, smem=()):
    return [
        pl.BlockSpec(memory_space=pltpu.SMEM) if i in smem else pl.BlockSpec(memory_space=pltpu.VMEM)
        for i in range(n)
    ]


def norm_rows(x, gain):
    mean = jnp.mean(x, axis=-1, keepdims=True)
    off = x - mean
    var = jnp.mean(off * off, axis=-1, keepdims=True)
    return off * lax.rsqrt(var + EPS) * gain


def dot_nt(a, b):
    return lax.dot_general(a, b, (((1,), (1,)), ((), ())), preferred_element_type=F32)


def dot_nn(a, b):
    return jnp.dot(a, b, preferred_element_type=F32)


def rows_to_tiles(rows, tiles, first):
    count = rows.shape[0]
    for c in range(8):
        tiles[pl.ds(first * 8 + c, count, stride=8), :] = rows[:, 128 * c : 128 * c + 128]


def tiles_to_rows(tiles, first, count):
    return [tiles[pl.ds(first * 8 + c, count, stride=8), :] for c in range(8)]


def attend_group(q, k, v, bias_of, extra, scale, store):
    lane_head = lax.broadcasted_iota(jnp.int32, (WT, 128), 1) // 32
    total = None
    for h in range(4):
        pick = lane_head == h
        qh = jnp.where(pick, q, jnp.zeros_like(q))
        vh = jnp.where(pick, v, jnp.zeros_like(v))
        s = dot_nt(qh, k) * scale + (bias_of(h) + extra)
        top = jnp.max(s, axis=-1, keepdims=True)
        p = jnp.exp(s - top)
        inv = 1.0 / jnp.sum(p, axis=-1, keepdims=True)
        o = dot_nn(p.astype(BF), vh) * inv
        total = o if total is None else total + o
    store(total)


def region_mask(thr):
    def reg(dim):
        t = lax.broadcasted_iota(jnp.int32, (WT, WT), dim)
        return jnp.where(t >= 72, t - 72, t) >= thr

    return jnp.where(reg(0) == reg(1), 0.0, NEG).astype(F32)


def frame_of(shift, window):
    ahead = shift <= window // 2
    return ahead, jnp.where(ahead, shift, shift - window)


def region_start(shift, up, band):
    return jnp.where(band == jnp.where(up, 7, 0), 12 * (6 - shift), 1000)


def fill_frame(up, right, own_ref, lon_ref, lat_ref, ext, ahead):
    lat_row = jnp.where(up == ahead, 15, 0)
    after = right == ahead
    for l in range(4):
        for r in range(12):
            ext[l, 3 + r, 6:18] = own_ref[l, r].astype(F32)
        for r in range(3):
            ext[l, lat_row + r, 6:18] = lat_ref[l, r, 0:12].astype(F32)

    def edge(cols):
        for l in range(4):
            for r in range(12):
                ext[l, 3 + r, cols] = lon_ref[l, r].astype(F32)
            for r in range(3):
                ext[l, lat_row + r, cols] = lat_ref[l, r, 12:18].astype(F32)

    @pl.when(after)
    def _():
        edge(slice(18, 24))

    @pl.when(jnp.logical_not(after))
    def _():
        edge(slice(0, 6))


def fine_attn_kernel(sc_ref, band_ref, own_ref, lon_ref, lat_ref, gain_ref, w_ref, bias_ref, out_ref, ext, xw, xn, q_s, k_s, v_s, mask_s, o_s):
    up, first_row = frame_of(sc_ref[0], 6)
    right, first_col = frame_of(sc_ref[1], 12)
    row0 = 3 + first_row
    turn = 18 - first_col
    fill_frame(up, right, own_ref, lon_ref, lat_ref, ext, True)
    for dp in range(2):
        for lr in range(2):
            for a in range(2):
                for b in range(6):
                    row = ((dp * 2 + lr) * 12 + a * 6 + b) * 12
                    full = ext[dp * 2 + a, row0 + lr * 6 + b]
                    xw[row : row + 12] = pltpu.roll(full, turn, 0)[0:12]
    gain = gain_ref[...]
    for i in range(4):
        xn[WT * i : WT * i + WT] = norm_rows(xw[WT * i : WT * i + WT], gain).astype(BF)
    place = lax.broadcasted_iota(jnp.int32, (384, 384), 1)
    source = ((place >> 5) & 3) * 96 + (place >> 7) * 32 + (place & 31)
    order = (lax.broadcasted_iota(jnp.int32, (384, 384), 0) == source).astype(F32).astype(BF)
    for j in range(4):
        cols = slice(128 * j, 128 * j + 128)
        w = dot_nn(w_ref[:, 384 * j : 384 * j + 384], order).astype(BF)
        y = dot_nn(xn[...], w).astype(BF)
        q_s[:, cols] = y[:, 0:128]
        k_s[:, cols] = y[:, 128:256]
        v_s[:, cols] = y[:, 256:384]

    def window(i, _):
        thr = jnp.where(i % 2 == jnp.where(up, 1, 0), region_start(sc_ref[0], up, band_ref[0]), 1000)
        mask_s[...] = region_mask(thr)
        rows = pl.ds(i * WT, WT)
        for j in range(4):
            cols = slice(128 * j, 128 * j + 128)

            def store(total, cols=cols):
                o_s[rows, cols] = total

            attend_group(
                q_s[rows, cols], k_s[rows, cols], v_s[rows, cols],
                lambda h, j=j: bias_ref[4 * j + h], mask_s[...], 32 ** (-0.5), store,
            )
        return 0

    lax.fori_loop(0, 4, window, 0)
    for dp in range(2):
        for lr in range(2):
            for a in range(2):
                for b in range(6):
                    row = ((dp * 2 + lr) * 12 + a * 6 + b) * 12
                    out_ref[dp * 2 + a, lr * 6 + b] = o_s[row : row + 12].astype(BF)


def fine_attention(scalars, band, own, lon, lat, gain, weights, bias):
    return pl.pallas_call(
        fine_attn_kernel,
        out_shape=jax.ShapeDtypeStruct((4, 12, 12, 512), BF),
        in_specs=full_spec(8, (0, 1)),
        out_specs=pl.BlockSpec(memory_space=pltpu.VMEM),
        scratch_shapes=[
            pltpu.VMEM((4, 18, 24, 512), F32),
            pltpu.VMEM((576, 512), F32),
            pltpu.VMEM((576, 512), BF),
            pltpu.VMEM((576, 512), BF),
            pltpu.VMEM((576, 512), BF),
            pltpu.VMEM((576, 512), BF),
            pltpu.VMEM((WT, WT), F32),
            pltpu.VMEM((576, 512), F32),
        ],
        compiler_params=pltpu.CompilerParams(vmem_limit_bytes=VLIM),
        name="fine_attention",
    )(scalars, band, own, lon, lat, gain, weights, bias)


def fine_post_kernel(sc_ref, own_ref, lon_ref, lat_ref, x_ref, wo_ref, g_ref, we_ref, wr_ref, mg_ref, wm_ref, fs_ref, ci_ref, ext, xf, mf, xp, mp, tiles):
    up, first_row = frame_of(sc_ref[0], 6)
    right, first_col = frame_of(sc_ref[1], 12)
    r0 = 3 - first_row
    turn = (18 + first_col) % 24
    fill_frame(up, right, own_ref, lon_ref, lat_ref, ext, False)
    for l in range(4):
        for r in range(12):
            own_x = x_ref[l, r].astype(F32)
            for c in range(4):
                xf[c, l, r, 0:12] = own_x[:, 128 * c : 128 * c + 128]
    for l in range(4):
        for r in range(12):
            turned = pltpu.roll(ext[l, r0 + r], turn, 0)[0:16]
            for c in range(4):
                mf[c, l, r] = turned[:, 128 * c : 128 * c + 128]
    for b in range(2):
        for a in range(2):
            for p in range(4):
                for i in range(6):
                    row = (2 * b + a) * WT + p * 36 + i * 6
                    for c in range(4):
                        cs = slice(128 * c, 128 * c + 128)
                        mp[row : row + 6, cs] = mf[c, p, 2 * i + a, pl.ds(b, 6, stride=2), :]
                        xp[row : row + 6, cs] = xf[c, p, 2 * i + a, pl.ds(b, 6, stride=2), :]
    gain = g_ref[...]
    def block(i, _):
        rows = pl.ds(i * WT, WT)
        att = (xp[rows] + dot_nn(mp[rows].astype(BF), wo_ref[...])).astype(BF).astype(F32)
        xn = norm_rows(att, gain).astype(BF)
        hid = jax.nn.gelu(dot_nn(xn, we_ref[...])).astype(BF)
        fs_ref[i] = (att + dot_nn(hid, wr_ref[...])).astype(BF)
        return 0

    lax.fori_loop(0, 4, block, 0)
    parts = [fs_ref[i].astype(F32) for i in range(4)]
    mean = sum(jnp.sum(v, axis=-1, keepdims=True) for v in parts) * (1.0 / 2048)
    parts = [v - mean for v in parts]
    var = sum(jnp.sum(v * v, axis=-1, keepdims=True) for v in parts) * (1.0 / 2048)
    inv = lax.rsqrt(var + EPS)
    acc = None
    for i in range(4):
        cs = slice(512 * i, 512 * i + 512)
        t = dot_nn((parts[i] * inv * mg_ref[:, cs]).astype(BF), wm_ref[cs, :])
        acc = t if acc is None else acc + t
    rows_to_tiles(acc, tiles, 0)
    ci_ref[...] = tiles[...].reshape(4, 6, 6, 8, 128).astype(BF)


def fine_post(scalars, own, lon, lat, field, wo, gain, we, wr, mg, wm):
    return pl.pallas_call(
        fine_post_kernel,
        out_shape=(jax.ShapeDtypeStruct((4, WT, 512), BF), jax.ShapeDtypeStruct((4, 6, 6, 8, 128), BF)),
        in_specs=full_spec(11, (0,)),
        out_specs=(pl.BlockSpec(memory_space=pltpu.VMEM), pl.BlockSpec(memory_space=pltpu.VMEM)),
        scratch_shapes=[
            pltpu.VMEM((4, 18, 24, 512), F32),
            pltpu.VMEM((4, 4, 12, 16, 128), F32),
            pltpu.VMEM((4, 4, 12, 16, 128), F32),
            pltpu.VMEM((576, 512), F32),
            pltpu.VMEM((576, 512), F32),
            pltpu.VMEM((WT * 8, 128), F32),
        ],
        compiler_params=pltpu.CompilerParams(vmem_limit_bytes=VLIM),
        name="fine_post",
    )(scalars, own, lon, lat, field, wo, gain, we, wr, mg, wm)


def coarse_attn_kernel(sc_ref, band_ref, own_ref, next_ref, gain_ref, g_ref, out_ref, ext, tiles, xf, xn, acc, mask_s):
    j = pl.program_id(0)

    @pl.when(j == 0)
    def _():
        right, first_col = frame_of(sc_ref[3], 12)
        up, _ = frame_of(sc_ref[2], 6)
        first = 6 + first_col
        edge = jnp.where(right, 18, 0)
        for a in range(2):
            for half in range(2):
                ext[a, :, 6 + 6 * half : 12 + 6 * half] = own_ref[half, a].astype(F32)
            for b in range(6):
                ext[a, b, pl.ds(edge, 6)] = next_ref[a, b].astype(F32)
        for a in range(2):
            for b in range(6):
                row = (a * 6 + b) * 96
                tiles[row : row + 96] = ext[a, b, pl.ds(first, 12)].reshape(96, 128)
        for c, part in enumerate(tiles_to_rows(tiles, 0, WT)):
            xf[:, 128 * c : 128 * c + 128] = part
        xn[...] = norm_rows(xf[...], gain_ref[...]).astype(BF)
        acc[...] = xf[...]
        mask_s[...] = region_mask(region_start(sc_ref[2], up, band_ref[0]))

    def rows_of(first, count):
        return jnp.concatenate([g_ref[0, first : first + count], g_ref[1, first : first + count]], axis=0)

    x = xn[...]
    q = dot_nt(x, rows_of(0, 64)).astype(BF)
    k = dot_nt(x, rows_of(64, 64)).astype(BF)
    v = dot_nt(x, rows_of(128, 64)).astype(BF)

    def bias_of(h):
        first = (h % 2) * 512
        hi = g_ref[h // 2, 256:400, first : first + WT].astype(F32)
        return hi + g_ref[h // 2, 256:400, first + 256 : first + 256 + WT].astype(F32)

    def store(total):
        acc[...] += dot_nn(total.astype(BF), rows_of(192, 64))

    attend_group(q, k, v, bias_of, mask_s[...], 32 ** (-0.5), store)

    @pl.when(j == 7)
    def _():
        rows_to_tiles(acc[...], tiles, 0)
        out_ref[...] = tiles[...].reshape(2, 6, 12, 8, 128).astype(BF)


def coarse_attention(scalars, band, own, ahead, gain, packed):
    vm = lambda: pl.BlockSpec(memory_space=pltpu.VMEM)
    return pl.pallas_call(
        coarse_attn_kernel,
        grid=(8,),
        out_shape=jax.ShapeDtypeStruct((2, 6, 12, 8, 128), BF),
        in_specs=[
            pl.BlockSpec(memory_space=pltpu.SMEM), pl.BlockSpec(memory_space=pltpu.SMEM), vm(), vm(), vm(),
            pl.BlockSpec((2, 400, 1024), lambda j: (j, 0, 0)),
        ],
        out_specs=vm(),
        scratch_shapes=[
            pltpu.VMEM((2, 6, 24, 8, 128), F32),
            pltpu.VMEM((WT * 8, 128), F32),
            pltpu.VMEM((WT, 1024), F32),
            pltpu.VMEM((WT, 1024), BF),
            pltpu.VMEM((WT, 1024), F32),
            pltpu.VMEM((WT, WT), F32),
        ],
        compiler_params=pltpu.CompilerParams(vmem_limit_bytes=VLIM, dimension_semantics=("arbitrary",)),
        name="coarse_attention",
    )(scalars, band, own, ahead, gain, packed)


def coarse_ff_kernel(own_ref, across_ref, mate_ref, gain_ref, g_ref, keep_ref, send_ref, tiles, xn, acc):
    sources = (own_ref[...], across_ref[...], mate_ref[0], mate_ref[1])
    for i, block in enumerate(sources):
        tiles[...] = block.astype(F32).reshape(WT * 8, 128)
        x = jnp.concatenate(tiles_to_rows(tiles, 0, WT), axis=1)
        xn[WT * i : WT * i + WT] = norm_rows(x, gain_ref[...]).astype(BF)
    for half in (1, 0):
        rows = slice(2 * WT * half, 2 * WT * half + 2 * WT)
        for i in range(4):
            hid = jax.nn.gelu(dot_nt(xn[rows], g_ref[i, 0:256])).astype(BF)
            part = dot_nn(hid, g_ref[i, 256:512])
            if i == 0:
                acc[...] = part
            else:
                acc[...] += part
        if half:
            send_ref[...] = acc[...].astype(BF)
        else:
            keep_ref[...] = acc[...]


def coarse_ff(own, across, mate, gain, packed):
    vm = lambda: pl.BlockSpec(memory_space=pltpu.VMEM)
    return pl.pallas_call(
        coarse_ff_kernel,
        out_shape=(jax.ShapeDtypeStruct((2 * WT, 1024), F32), jax.ShapeDtypeStruct((2 * WT, 1024), BF)),
        in_specs=full_spec(5),
        out_specs=(vm(), vm()),
        scratch_shapes=[
            pltpu.VMEM((WT * 8, 128), F32),
            pltpu.VMEM((4 * WT, 1024), BF),
            pltpu.VMEM((2 * WT, 1024), F32),
        ],
        compiler_params=pltpu.CompilerParams(vmem_limit_bytes=VLIM),
        name="coarse_ff",
    )(own, across, mate, gain, packed)


def blend_kernel(mid_ref, keep_ref, mate_ref, across_ref, wu_ref, fs_ref, out_ref, cs_ref, tiles, rows_s, grid_s):
    tiles[...] = mid_ref[...].astype(F32).reshape(WT * 8, 128)
    mid = jnp.concatenate(tiles_to_rows(tiles, 0, WT), axis=1)
    added = keep_ref[0:WT] + mate_ref[0:WT].astype(F32) + across_ref[...].astype(F32)
    rows_s[...] = mid + added
    state = rows_s[...].astype(BF)
    for p in range(4):
        for i in range(6):
            row = p * 36 + i * 6
            cs_ref[p, i] = rows_s[row : row + 6].astype(BF)
    for blk in range(4):
        b, a = blk // 2, blk % 2
        e = dot_nn(state, wu_ref[:, 512 * blk : 512 * blk + 512])
        t = fs_ref[blk].astype(F32) + e
        for p in range(4):
            for i in range(6):
                row = p * 36 + i * 6
                for c in range(4):
                    cs = slice(128 * c, 128 * c + 128)
                    grid_s[c, p, 2 * i + a, pl.ds(b, 6, stride=2), :] = t[row : row + 6, cs]
    for p in range(4):
        for r in range(12):
            for c in range(4):
                out_ref[p, r, :, 128 * c : 128 * c + 128] = grid_s[c, p, r, 0:12].astype(BF)


def blend(mid, keep, mate, across, wu, fs):
    return pl.pallas_call(
        blend_kernel,
        out_shape=(jax.ShapeDtypeStruct((4, 12, 12, 512), BF), jax.ShapeDtypeStruct((4, 6, 6, 1024), BF)),
        in_specs=full_spec(6),
        out_specs=(pl.BlockSpec(memory_space=pltpu.VMEM), pl.BlockSpec(memory_space=pltpu.VMEM)),
        scratch_shapes=[
            pltpu.VMEM((WT * 8, 128), F32),
            pltpu.VMEM((WT, 1024), F32),
            pltpu.VMEM((4, 4, 12, 16, 128), F32),
        ],
        compiler_params=pltpu.CompilerParams(vmem_limit_bytes=VLIM),
        name="blend",
    )(mid, keep, mate, across, wu, fs)


WL = 6
WW = 12


def shifted(block, axis, distance):
    devices = range(lax.axis_size(axis))
    route = [((i - distance) % len(devices), i) for i in devices]
    return lax.ppermute(block, axis, route)


def swapped(block, bit):
    return lax.ppermute(block, "lon", [(i, i ^ bit) for i in range(lax.axis_size("lon"))])


def chip_shifted(block, distance):
    count = lax.axis_size("lon")
    return lax.ppermute(block, "lon", [((i - 2 * distance) % count, i) for i in range(count)])


def fine_shift_lon(block, distance):
    return shifted(block, "lon", distance)


def fine_shift_lat(block, distance):
    return shifted(block, "lat", distance)


LAT_PLAN = ((1, 1), (1, 2), (1, 3), (-1, 2), (-1, 1))
LON_PLAN = ((1, 1), (1, 3), (1, 6), (-1, 6), (-1, 3), (-1, 1))


def halo(choice, plan, low, high, dim, full, move, to_frame):
    def branch(side, width):
        def send(edges):
            if side == (1 if to_frame else -1):
                piece = move(lax.slice_in_dim(edges[0], 0, width, axis=dim), -1)
                room = (0, full - width)
            else:
                size = edges[1].shape[dim]
                piece = move(lax.slice_in_dim(edges[1], size - width, size, axis=dim), 1)
                room = (full - width, 0)
            return jnp.pad(piece, [room if i == dim else (0, 0) for i in range(piece.ndim)])

        return send

    return lax.switch(choice, [branch(*entry) for entry in plan], (low, high))


def fine_rows(choice, low, high, piece, to_frame):
    def move(edges, distance):
        return fine_shift_lat(jnp.concatenate(edges, axis=2), distance)

    def branch(side, width):
        def send(pair):
            if side == (1 if to_frame else -1):
                return jnp.pad(move([pair[0][:, :width], pair[2][:, :width]], -1), ((0, 0), (0, 3 - width), (0, 0), (0, 0)))
            return jnp.pad(move([pair[1][:, -width:], pair[2][:, -width:]], 1), ((0, 0), (3 - width, 0), (0, 0), (0, 0)))

        return send

    return lax.switch(choice, [branch(*entry) for entry in LAT_PLAN], (low, high, piece))


def plan_choice(shift, steps):
    return sum((shift >= step).astype(jnp.int32) for step in steps)


def in_order(core, mine, other):
    first = jnp.where(core == 0, mine, other)
    second = jnp.where(core == 0, other, mine)
    return jnp.stack([first, second])


def pack_attention(triple, output, bias):
    wide = triple.shape[0]
    columns = triple.reshape(wide, 2, 3, 32).transpose(2, 1, 3, 0).reshape(192, wide)
    padded = jnp.pad(bias, ((0, 0), (0, 0), (0, 256 - WT)))
    high = lax.reduce_precision(padded, 8, 7)
    low = padded - high
    both = jnp.stack([high, low], axis=1).astype(BF).transpose(2, 0, 1, 3).reshape(WT, 1024)
    return jnp.concatenate([columns, output, both], axis=0)


def body(
    fine_field,
    offsets,
    fine_prenorm,
    fine_triple,
    fine_bias,
    fine_output,
    fine_midnorm,
    fine_expand,
    fine_reduce,
    merge_gain,
    merge_weight,
    coarse_prenorm,
    coarse_triple,
    coarse_bias,
    coarse_output,
    coarse_midnorm,
    coarse_expand,
    coarse_reduce,
    upsample_weight,
):
    levels, lat_rows, lon_cols, channels = fine_field.shape
    lat_count = lax.axis_size("lat")
    lat_index = lax.axis_index("lat")
    fine_lat, fine_lon, coarse_lat, coarse_lon = [jnp.maximum(offsets[i], 1) for i in range(4)]
    band = lat_index.astype(jnp.int32).reshape(1)
    core = lax.axis_index("lon") % 2
    coarse_row = frame_of(coarse_lat, WL)[1]
    coarse_col = frame_of(coarse_lon, WW)[1]
    fine_lat_plan = plan_choice(fine_lat, (2, 3, 4, 5))
    fine_lon_plan = plan_choice(fine_lon, (2, 4, 7, 9, 11))
    coarse_lat_plan = plan_choice(coarse_lat, (2, 3, 4, 5))
    coarse_lon_plan = plan_choice(coarse_lon, (2, 4, 7, 9, 11))
    attn_pack = pack_attention(coarse_triple, coarse_output, coarse_bias)
    low_rows, high_rows = fine_field[:, :3], fine_field[:, -3:]
    attn_all = lax.all_gather(attn_pack, "lon", axis=0, tiled=False)
    ff_pack = jnp.concatenate([coarse_expand.T, coarse_reduce], axis=0)
    rings = [[z * 8 + y * 2 + c for y in range(4)] for z in range(2) for c in range(2)]
    ff_all = lax.all_gather(ff_pack, "lon", axis=0, tiled=False, axis_index_groups=rings)
    lon_piece = halo(
        fine_lon_plan, LON_PLAN, fine_field[:, :, :6], fine_field[:, :, -6:], 2, 6, fine_shift_lon, True
    )
    lat_piece = fine_rows(fine_lat_plan, low_rows, high_rows, lon_piece, True)
    half_rows = lat_rows // 2
    half_cols = lon_cols // 2

    mixed_fine = fine_attention(
        offsets, band, fine_field, lon_piece, lat_piece, fine_prenorm[None], fine_triple, fine_bias
    )
    lon_piece = halo(fine_lon_plan, LON_PLAN, mixed_fine, mixed_fine, 2, 6, fine_shift_lon, False)
    lat_piece = fine_rows(fine_lat_plan, mixed_fine, mixed_fine, lon_piece, False)
    fine_state, coarse_own = fine_post(
        offsets, mixed_fine, lon_piece, lat_piece, fine_field, fine_output, fine_midnorm[None],
        fine_expand, fine_reduce, merge_gain[None], merge_weight,
    )
    rows_piece = halo(coarse_lat_plan, LAT_PLAN, coarse_own, coarse_own, 1, 3, fine_shift_lat, True)
    framed = lax.dynamic_slice_in_dim(
        jnp.concatenate([rows_piece, coarse_own, rows_piece], axis=1), 3 + coarse_row, half_rows, axis=1
    )
    mine = lax.dynamic_slice_in_dim(framed, 2 * core, 2, axis=0)
    other = swapped(lax.dynamic_slice_in_dim(framed, 2 - 2 * core, 2, axis=0), 1)
    chip = in_order(core, mine, other)
    chip_piece = halo(coarse_lon_plan, LON_PLAN, chip[0], chip[1], 2, 6, chip_shifted, True)
    mid_framed = coarse_attention(offsets, band, chip, chip_piece, coarse_prenorm[None], attn_all)
    cols_piece = halo(coarse_lon_plan, LON_PLAN, mid_framed, mid_framed, 2, 6, chip_shifted, False)
    spread = jnp.concatenate([cols_piece, mid_framed, cols_piece], axis=2)
    first = 6 - coarse_col
    mine = lax.dynamic_slice_in_dim(spread, first + half_cols * core, half_cols, axis=2)
    other = swapped(
        lax.dynamic_slice_in_dim(spread, first + half_cols * (1 - core), half_cols, axis=2), 1
    )
    levels_all = in_order(core, mine, other).reshape(levels, half_rows, half_cols, 8, 128)
    rows_piece = halo(coarse_lat_plan, LAT_PLAN, levels_all, levels_all, 1, 3, fine_shift_lat, False)
    mid_own = lax.dynamic_slice_in_dim(
        jnp.concatenate([rows_piece, levels_all, rows_piece], axis=1), 3 - coarse_row, half_rows, axis=1
    )
    mid_own = mid_own.reshape(WT, 8, 128)
    across = swapped(mid_own, 8)
    mate = swapped(jnp.stack([mid_own, across]), 1)
    keep, send = coarse_ff(mid_own, across, mate, coarse_midnorm[None], ff_all)
    from_mate = swapped(send, 1)
    from_across = swapped((keep[WT:] + from_mate[WT:].astype(F32)).astype(BF), 8)
    return blend(mid_own, keep, from_mate, from_across, upsample_weight, fine_state)


def solution(mesh):
    placed = (
        P(None, "lat", "lon", None),
        P(),
        P(),
        P(),
        P(),
        P(),
        P(),
        P(),
        P(),
        P(),
        P(),
        P(),
        P(None, "lon"),
        P("lon", None, None),
        P("lon", None),
        P(),
        P(None, "lon"),
        P("lon", None),
        P(),
    )
    return jax.shard_map(
        body,
        mesh=mesh,
        in_specs=placed,
        out_specs=(P(None, "lat", "lon", None), P(None, "lat", "lon", None)),
        check_vma=False,
    )
```

```python
import jax
import jax.numpy as jnp
from jax import lax
from jax.sharding import PartitionSpec as P
from jax.experimental import pallas as pl
from jax.experimental.pallas import tpu as pltpu

BF = jnp.bfloat16
F32 = jnp.float32
EPS = 1e-05
NEG = -1e30
WT = 144
MIB = 1024 * 1024


def full_spec(n, smem=(), hbm=()):
    def space(i):
        return pltpu.SMEM if i in smem else pltpu.HBM if i in hbm else pltpu.VMEM

    return [pl.BlockSpec(memory_space=space(i)) for i in range(n)]


def in_hbm(array):
    return pltpu.with_memory_space_constraint(array, pltpu.HBM)


def norm_rows(x, gain):
    mean = jnp.mean(x, axis=-1, keepdims=True)
    off = x - mean
    var = jnp.mean(off * off, axis=-1, keepdims=True)
    return off * lax.rsqrt(var + EPS) * gain


def dot_nt(a, b):
    return lax.dot_general(a, b, (((1,), (1,)), ((), ())), preferred_element_type=F32)


def dot_nn(a, b):
    return jnp.dot(a, b, preferred_element_type=F32)


def rows_to_tiles(rows, tiles, first):
    count = rows.shape[0]
    for c in range(8):
        tiles[pl.ds(first * 8 + c, count, stride=8), :] = rows[:, 128 * c : 128 * c + 128]


def tiles_to_rows(tiles, first, count):
    return [tiles[pl.ds(first * 8 + c, count, stride=8), :] for c in range(8)]


def attend_group(q, k, v, bias_of, extra, scale, store):
    lane_head = lax.broadcasted_iota(jnp.int32, (WT, 128), 1) // 32
    total = None
    for h in range(4):
        pick = lane_head == h
        qh = jnp.where(pick, q, jnp.zeros_like(q))
        vh = jnp.where(pick, v, jnp.zeros_like(v))
        s = dot_nt(qh, k) * scale + (bias_of(h) + extra)
        top = jnp.max(s, axis=-1, keepdims=True)
        p = jnp.exp(s - top)
        inv = 1.0 / jnp.sum(p, axis=-1, keepdims=True)
        o = dot_nn(p.astype(BF), vh) * inv
        total = o if total is None else total + o
    store(total)


def region_mask(thr):
    def reg(dim):
        t = lax.broadcasted_iota(jnp.int32, (WT, WT), dim)
        return jnp.where(t >= 72, t - 72, t) >= thr

    return jnp.where(reg(0) == reg(1), 0.0, NEG).astype(F32)


def frame_of(shift, window):
    ahead = shift <= window // 2
    return ahead, jnp.where(ahead, shift, shift - window)


def region_start(shift, up, band):
    return jnp.where(band == jnp.where(up, 7, 0), 12 * (6 - shift), 1000)


def fill_frame(up, right, own_ref, lon_ref, lat_ref, ext, ahead):
    lat_row = jnp.where(up == ahead, 15, 0)
    after = right == ahead
    for l in range(4):
        for r in range(12):
            ext[l, 3 + r, 6:18] = own_ref[l, r].astype(F32)
        for r in range(3):
            ext[l, lat_row + r, 6:18] = lat_ref[l, r, 0:12].astype(F32)

    def edge(cols):
        for l in range(4):
            for r in range(12):
                ext[l, 3 + r, cols] = lon_ref[l, r].astype(F32)
            for r in range(3):
                ext[l, lat_row + r, cols] = lat_ref[l, r, 12:18].astype(F32)

    @pl.when(after)
    def _():
        edge(slice(18, 24))

    @pl.when(jnp.logical_not(after))
    def _():
        edge(slice(0, 6))


def fine_attn_kernel(sc_ref, band_ref, own_ref, lon_ref, lat_ref, gain_ref, w_hbm, bias_ref, out_ref, ext, xw, xn, q_s, k_s, v_s, mask_s, o_s, w_ref, sem):
    fetch = pltpu.make_async_copy(w_hbm, w_ref, sem.at[0])
    fetch.start()
    up, first_row = frame_of(sc_ref[0], 6)
    right, first_col = frame_of(sc_ref[1], 12)
    row0 = 3 + first_row
    turn = 18 - first_col
    fill_frame(up, right, own_ref, lon_ref, lat_ref, ext, True)
    for dp in range(2):
        for lr in range(2):
            for a in range(2):
                for b in range(6):
                    row = ((dp * 2 + lr) * 12 + a * 6 + b) * 12
                    full = ext[dp * 2 + a, row0 + lr * 6 + b]
                    xw[row : row + 12] = pltpu.roll(full, turn, 0)[0:12]
    gain = gain_ref[...]
    for i in range(4):
        xn[WT * i : WT * i + WT] = norm_rows(xw[WT * i : WT * i + WT], gain).astype(BF)
    place = lax.broadcasted_iota(jnp.int32, (384, 384), 1)
    source = ((place >> 5) & 3) * 96 + (place >> 7) * 32 + (place & 31)
    order = (lax.broadcasted_iota(jnp.int32, (384, 384), 0) == source).astype(F32).astype(BF)
    fetch.wait()
    for j in range(4):
        cols = slice(128 * j, 128 * j + 128)
        w = dot_nn(w_ref[:, 384 * j : 384 * j + 384], order).astype(BF)
        y = dot_nn(xn[...], w).astype(BF)
        q_s[:, cols] = y[:, 0:128]
        k_s[:, cols] = y[:, 128:256]
        v_s[:, cols] = y[:, 256:384]

    def window(i, _):
        thr = jnp.where(i % 2 == jnp.where(up, 1, 0), region_start(sc_ref[0], up, band_ref[0]), 1000)
        mask_s[...] = region_mask(thr)
        rows = pl.ds(i * WT, WT)
        for j in range(4):
            cols = slice(128 * j, 128 * j + 128)

            def store(total, cols=cols):
                o_s[rows, cols] = total

            attend_group(
                q_s[rows, cols], k_s[rows, cols], v_s[rows, cols],
                lambda h, j=j: bias_ref[4 * j + h], mask_s[...], 32 ** (-0.5), store,
            )
        return 0

    lax.fori_loop(0, 4, window, 0)
    for dp in range(2):
        for lr in range(2):
            for a in range(2):
                for b in range(6):
                    row = ((dp * 2 + lr) * 12 + a * 6 + b) * 12
                    out_ref[dp * 2 + a, lr * 6 + b] = o_s[row : row + 12].astype(BF)


def fine_attention(scalars, band, own, lon, lat, gain, weights, bias):
    return pl.pallas_call(
        fine_attn_kernel,
        out_shape=jax.ShapeDtypeStruct((4, 12, 12, 512), BF),
        in_specs=full_spec(8, (0, 1), (6,)),
        out_specs=pl.BlockSpec(memory_space=pltpu.VMEM),
        scratch_shapes=[
            pltpu.VMEM((4, 18, 24, 512), F32),
            pltpu.VMEM((576, 512), F32),
            pltpu.VMEM((576, 512), BF),
            pltpu.VMEM((576, 512), BF),
            pltpu.VMEM((576, 512), BF),
            pltpu.VMEM((576, 512), BF),
            pltpu.VMEM((WT, WT), F32),
            pltpu.VMEM((576, 512), F32),
            pltpu.VMEM((512, 1536), BF),
            pltpu.SemaphoreType.DMA((1,)),
        ],
        compiler_params=pltpu.CompilerParams(vmem_limit_bytes=20 * MIB),
        name="fine_attention",
    )(scalars, band, own, lon, lat, gain, in_hbm(weights), bias)


def fine_post_kernel(sc_ref, own_ref, lon_ref, lat_ref, x_ref, wo_ref, g_ref, we_ref, wr_hbm, mg_ref, wm_hbm, fs_ref, ci_ref, ext, xf, mf, xp, mp, tiles, wr_ref, wm_ref, sem):
    fetch_reduce = pltpu.make_async_copy(wr_hbm, wr_ref, sem.at[0])
    fetch_merge = pltpu.make_async_copy(wm_hbm, wm_ref, sem.at[1])
    fetch_reduce.start()
    fetch_merge.start()
    up, first_row = frame_of(sc_ref[0], 6)
    right, first_col = frame_of(sc_ref[1], 12)
    r0 = 3 - first_row
    turn = (18 + first_col) % 24
    fill_frame(up, right, own_ref, lon_ref, lat_ref, ext, False)
    for l in range(4):
        for r in range(12):
            own_x = x_ref[l, r].astype(F32)
            for c in range(4):
                xf[c, l, r, 0:12] = own_x[:, 128 * c : 128 * c + 128]
    for l in range(4):
        for r in range(12):
            turned = pltpu.roll(ext[l, r0 + r], turn, 0)[0:16]
            for c in range(4):
                mf[c, l, r] = turned[:, 128 * c : 128 * c + 128]
    for b in range(2):
        for a in range(2):
            for p in range(4):
                for i in range(6):
                    row = (2 * b + a) * WT + p * 36 + i * 6
                    for c in range(4):
                        cs = slice(128 * c, 128 * c + 128)
                        mp[row : row + 6, cs] = mf[c, p, 2 * i + a, pl.ds(b, 6, stride=2), :]
                        xp[row : row + 6, cs] = xf[c, p, 2 * i + a, pl.ds(b, 6, stride=2), :]
    fetch_reduce.wait()
    gain = g_ref[...]

    def block(i, _):
        rows = pl.ds(i * WT, WT)
        att = (xp[rows] + dot_nn(mp[rows].astype(BF), wo_ref[...])).astype(BF).astype(F32)
        xn = norm_rows(att, gain).astype(BF)
        hid = jax.nn.gelu(dot_nn(xn, we_ref[...])).astype(BF)
        fs_ref[i] = (att + dot_nn(hid, wr_ref[...])).astype(BF)
        return 0

    lax.fori_loop(0, 4, block, 0)
    fetch_merge.wait()
    parts = [fs_ref[i].astype(F32) for i in range(4)]
    mean = sum(jnp.sum(v, axis=-1, keepdims=True) for v in parts) * (1.0 / 2048)
    parts = [v - mean for v in parts]
    var = sum(jnp.sum(v * v, axis=-1, keepdims=True) for v in parts) * (1.0 / 2048)
    inv = lax.rsqrt(var + EPS)
    acc = None
    for i in range(4):
        cs = slice(512 * i, 512 * i + 512)
        t = dot_nn((parts[i] * inv * mg_ref[:, cs]).astype(BF), wm_ref[cs, :])
        acc = t if acc is None else acc + t
    rows_to_tiles(acc, tiles, 0)
    ci_ref[...] = tiles[...].reshape(4, 6, 6, 8, 128).astype(BF)


def fine_post(scalars, own, lon, lat, field, wo, gain, we, wr, mg, wm):
    return pl.pallas_call(
        fine_post_kernel,
        out_shape=(jax.ShapeDtypeStruct((4, WT, 512), BF), jax.ShapeDtypeStruct((4, 6, 6, 8, 128), BF)),
        in_specs=full_spec(11, (0,), (8, 10)),
        out_specs=(pl.BlockSpec(memory_space=pltpu.VMEM), pl.BlockSpec(memory_space=pltpu.VMEM)),
        scratch_shapes=[
            pltpu.VMEM((4, 18, 24, 512), F32),
            pltpu.VMEM((4, 4, 12, 16, 128), F32),
            pltpu.VMEM((4, 4, 12, 16, 128), F32),
            pltpu.VMEM((576, 512), F32),
            pltpu.VMEM((576, 512), F32),
            pltpu.VMEM((WT * 8, 128), F32),
            pltpu.VMEM((2048, 512), BF),
            pltpu.VMEM((2048, 1024), BF),
            pltpu.SemaphoreType.DMA((2,)),
        ],
        compiler_params=pltpu.CompilerParams(vmem_limit_bytes=30 * MIB),
        name="fine_post",
    )(scalars, own, lon, lat, field, wo, gain, we, in_hbm(wr), mg, in_hbm(wm))


def coarse_attn_kernel(sc_ref, band_ref, own_ref, next_ref, gain_ref, g_ref, out_ref, ext, tiles, xf, xn, acc, mask_s):
    j = pl.program_id(0)

    @pl.when(j == 0)
    def _():
        right, first_col = frame_of(sc_ref[3], 12)
        up, _ = frame_of(sc_ref[2], 6)
        first = 6 + first_col
        edge = jnp.where(right, 18, 0)
        for a in range(2):
            for half in range(2):
                ext[a, :, 6 + 6 * half : 12 + 6 * half] = own_ref[half, a].astype(F32)
            for b in range(6):
                ext[a, b, pl.ds(edge, 6)] = next_ref[a, b].astype(F32)
        for a in range(2):
            for b in range(6):
                row = (a * 6 + b) * 96
                tiles[row : row + 96] = ext[a, b, pl.ds(first, 12)].reshape(96, 128)
        for c, part in enumerate(tiles_to_rows(tiles, 0, WT)):
            xf[:, 128 * c : 128 * c + 128] = part
        xn[...] = norm_rows(xf[...], gain_ref[...]).astype(BF)
        acc[...] = xf[...]
        mask_s[...] = region_mask(region_start(sc_ref[2], up, band_ref[0]))

    def rows_of(first, count):
        return jnp.concatenate([g_ref[0, first : first + count], g_ref[1, first : first + count]], axis=0)

    x = xn[...]
    q = dot_nt(x, rows_of(0, 64)).astype(BF)
    k = dot_nt(x, rows_of(64, 64)).astype(BF)
    v = dot_nt(x, rows_of(128, 64)).astype(BF)

    def bias_of(h):
        def main(part):
            first = (h % 2) * 256 + part * 128
            halves = [g_ref[h // 2, 272:344, first + 512 * i : first + 512 * i + 128].astype(F32) for i in range(2)]
            return jnp.concatenate(halves, axis=0)

        def tail(part):
            first = (h % 2) * 512 + part * 256
            return g_ref[h // 2, 256:272, first : first + 256].astype(F32)

        edge = jnp.transpose(tail(0) + tail(1))[:WT]
        return jnp.concatenate([main(0) + main(1), edge], axis=1)

    def store(total):
        acc[...] += dot_nn(total.astype(BF), rows_of(192, 64))

    attend_group(q, k, v, bias_of, mask_s[...], 32 ** (-0.5), store)

    @pl.when(j == 7)
    def _():
        rows_to_tiles(acc[...], tiles, 0)
        out_ref[...] = tiles[...].reshape(2, 6, 12, 8, 128).astype(BF)


def coarse_attention(scalars, band, own, ahead, gain, packed):
    vm = lambda: pl.BlockSpec(memory_space=pltpu.VMEM)
    return pl.pallas_call(
        coarse_attn_kernel,
        grid=(8,),
        out_shape=jax.ShapeDtypeStruct((2, 6, 12, 8, 128), BF),
        in_specs=[
            pl.BlockSpec(memory_space=pltpu.SMEM), pl.BlockSpec(memory_space=pltpu.SMEM), vm(), vm(), vm(),
            pl.BlockSpec((2, 344, 1024), lambda j: (j, 0, 0)),
        ],
        out_specs=vm(),
        scratch_shapes=[
            pltpu.VMEM((2, 6, 24, 8, 128), F32),
            pltpu.VMEM((WT * 8, 128), F32),
            pltpu.VMEM((WT, 1024), F32),
            pltpu.VMEM((WT, 1024), BF),
            pltpu.VMEM((WT, 1024), F32),
            pltpu.VMEM((WT, WT), F32),
        ],
        compiler_params=pltpu.CompilerParams(vmem_limit_bytes=56 * MIB, dimension_semantics=("arbitrary",)),
        name="coarse_attention",
    )(scalars, band, own, ahead, gain, packed)


def coarse_ff_kernel(own_ref, across_ref, mate_ref, gain_ref, g_hbm, keep_ref, send_ref, tiles, xn, acc, g_ref, sem):
    fetches = [pltpu.make_async_copy(g_hbm.at[i], g_ref.at[i], sem.at[i]) for i in range(4)]
    for fetch in fetches:
        fetch.start()
    sources = (own_ref[...], across_ref[...], mate_ref[0], mate_ref[1])
    for i, block in enumerate(sources):
        tiles[...] = block.astype(F32).reshape(WT * 8, 128)
        x = jnp.concatenate(tiles_to_rows(tiles, 0, WT), axis=1)
        xn[WT * i : WT * i + WT] = norm_rows(x, gain_ref[...]).astype(BF)
    for half in (1, 0):
        rows = slice(2 * WT * half, 2 * WT * half + 2 * WT)
        for i in range(4):
            if half:
                fetches[i].wait()
            hid = jax.nn.gelu(dot_nt(xn[rows], g_ref[i, 0:256])).astype(BF)
            part = dot_nn(hid, g_ref[i, 256:512])
            if i == 0:
                acc[...] = part
            else:
                acc[...] += part
        if half:
            send_ref[...] = acc[...].astype(BF)
        else:
            keep_ref[...] = acc[...]


def coarse_ff(own, across, mate, gain, packed):
    vm = lambda: pl.BlockSpec(memory_space=pltpu.VMEM)
    return pl.pallas_call(
        coarse_ff_kernel,
        out_shape=(jax.ShapeDtypeStruct((2 * WT, 1024), F32), jax.ShapeDtypeStruct((2 * WT, 1024), BF)),
        in_specs=full_spec(5, (), (4,)),
        out_specs=(vm(), vm()),
        scratch_shapes=[
            pltpu.VMEM((WT * 8, 128), F32),
            pltpu.VMEM((4 * WT, 1024), BF),
            pltpu.VMEM((2 * WT, 1024), F32),
            pltpu.VMEM((4, 512, 1024), BF),
            pltpu.SemaphoreType.DMA((4,)),
        ],
        compiler_params=pltpu.CompilerParams(vmem_limit_bytes=20 * MIB),
        name="coarse_ff",
    )(own, across, mate, gain, in_hbm(packed))


def blend_kernel(mid_ref, keep_ref, mate_ref, across_ref, wu_ref, fs_ref, out_ref, cs_ref, tiles, rows_s, grid_s):
    tiles[...] = mid_ref[...].astype(F32).reshape(WT * 8, 128)
    mid = jnp.concatenate(tiles_to_rows(tiles, 0, WT), axis=1)
    added = keep_ref[0:WT] + mate_ref[0:WT].astype(F32) + across_ref[...].astype(F32)
    rows_s[...] = mid + added
    state = rows_s[...].astype(BF)
    for p in range(4):
        for i in range(6):
            row = p * 36 + i * 6
            cs_ref[p, i] = rows_s[row : row + 6].astype(BF)
    for blk in range(4):
        b, a = blk // 2, blk % 2
        e = dot_nn(state, wu_ref[:, 512 * blk : 512 * blk + 512])
        t = fs_ref[blk].astype(F32) + e
        for p in range(4):
            for i in range(6):
                row = p * 36 + i * 6
                for c in range(4):
                    cs = slice(128 * c, 128 * c + 128)
                    grid_s[c, p, 2 * i + a, pl.ds(b, 6, stride=2), :] = t[row : row + 6, cs]
    for p in range(4):
        for r in range(12):
            for c in range(4):
                out_ref[p, r, :, 128 * c : 128 * c + 128] = grid_s[c, p, r, 0:12].astype(BF)


def blend(mid, keep, mate, across, wu, fs):
    return pl.pallas_call(
        blend_kernel,
        out_shape=(jax.ShapeDtypeStruct((4, 12, 12, 512), BF), jax.ShapeDtypeStruct((4, 6, 6, 1024), BF)),
        in_specs=full_spec(6),
        out_specs=(pl.BlockSpec(memory_space=pltpu.VMEM), pl.BlockSpec(memory_space=pltpu.VMEM)),
        scratch_shapes=[
            pltpu.VMEM((WT * 8, 128), F32),
            pltpu.VMEM((WT, 1024), F32),
            pltpu.VMEM((4, 4, 12, 16, 128), F32),
        ],
        compiler_params=pltpu.CompilerParams(vmem_limit_bytes=20 * MIB),
        name="blend",
    )(mid, keep, mate, across, wu, fs)


WL = 6
WW = 12


def shifted(block, axis, distance):
    devices = range(lax.axis_size(axis))
    route = [((i - distance) % len(devices), i) for i in devices]
    return lax.ppermute(block, axis, route)


def swapped(block, bit):
    return lax.ppermute(block, "lon", [(i, i ^ bit) for i in range(lax.axis_size("lon"))])


def chip_shifted(block, distance):
    count = lax.axis_size("lon")
    return lax.ppermute(block, "lon", [((i - 2 * distance) % count, i) for i in range(count)])


def fine_shift_lon(block, distance):
    return shifted(block, "lon", distance)


def fine_shift_lat(block, distance):
    return shifted(block, "lat", distance)


LAT_PLAN = ((1, 1), (1, 2), (1, 3), (-1, 2), (-1, 1))
LON_PLAN = ((1, 1), (1, 3), (1, 6), (-1, 6), (-1, 3), (-1, 1))


def halo(choice, plan, low, high, dim, full, move, to_frame):
    def branch(side, width):
        def send(edges):
            if side == (1 if to_frame else -1):
                piece = move(lax.slice_in_dim(edges[0], 0, width, axis=dim), -1)
                room = (0, full - width)
            else:
                size = edges[1].shape[dim]
                piece = move(lax.slice_in_dim(edges[1], size - width, size, axis=dim), 1)
                room = (full - width, 0)
            return jnp.pad(piece, [room if i == dim else (0, 0) for i in range(piece.ndim)])

        return send

    return lax.switch(choice, [branch(*entry) for entry in plan], (low, high))


def fine_rows(choice, low, high, piece, to_frame):
    def move(edges, distance):
        return fine_shift_lat(jnp.concatenate(edges, axis=2), distance)

    def branch(side, width):
        def send(pair):
            if side == (1 if to_frame else -1):
                return jnp.pad(move([pair[0][:, :width], pair[2][:, :width]], -1), ((0, 0), (0, 3 - width), (0, 0), (0, 0)))
            return jnp.pad(move([pair[1][:, -width:], pair[2][:, -width:]], 1), ((0, 0), (3 - width, 0), (0, 0), (0, 0)))

        return send

    return lax.switch(choice, [branch(*entry) for entry in LAT_PLAN], (low, high, piece))


def plan_choice(shift, steps):
    return sum((shift >= step).astype(jnp.int32) for step in steps)


def in_order(core, mine, other):
    first = jnp.where(core == 0, mine, other)
    second = jnp.where(core == 0, other, mine)
    return jnp.stack([first, second])


def pack_attention(triple, output, bias):
    wide = triple.shape[0]
    columns = triple.reshape(wide, 2, 3, 32).transpose(2, 1, 3, 0).reshape(192, wide)
    high = lax.reduce_precision(bias, 8, 7)
    both = jnp.stack([high, bias - high], axis=1).astype(BF)
    tail = jnp.pad(both[..., 128:].transpose(3, 0, 1, 2), ((0, 0), (0, 0), (0, 0), (0, 256 - WT)))
    main = both[..., :128].reshape(2, 2, 2, 72, 128).transpose(3, 2, 0, 1, 4)
    return jnp.concatenate([columns, output, tail.reshape(16, 1024), main.reshape(72, 1024)], axis=0)


def body(
    fine_field,
    offsets,
    fine_prenorm,
    fine_triple,
    fine_bias,
    fine_output,
    fine_midnorm,
    fine_expand,
    fine_reduce,
    merge_gain,
    merge_weight,
    coarse_prenorm,
    coarse_triple,
    coarse_bias,
    coarse_output,
    coarse_midnorm,
    coarse_expand,
    coarse_reduce,
    upsample_weight,
):
    levels, lat_rows, lon_cols, channels = fine_field.shape
    lat_count = lax.axis_size("lat")
    lat_index = lax.axis_index("lat")
    fine_lat, fine_lon, coarse_lat, coarse_lon = [jnp.maximum(offsets[i], 1) for i in range(4)]
    band = lat_index.astype(jnp.int32).reshape(1)
    core = lax.axis_index("lon") % 2
    coarse_row = frame_of(coarse_lat, WL)[1]
    coarse_col = frame_of(coarse_lon, WW)[1]
    fine_lat_plan = plan_choice(fine_lat, (2, 3, 4, 5))
    fine_lon_plan = plan_choice(fine_lon, (2, 4, 7, 9, 11))
    coarse_lat_plan = plan_choice(coarse_lat, (2, 3, 4, 5))
    coarse_lon_plan = plan_choice(coarse_lon, (2, 4, 7, 9, 11))
    attn_pack = pack_attention(coarse_triple, coarse_output, coarse_bias)
    low_rows, high_rows = fine_field[:, :3], fine_field[:, -3:]
    attn_all = lax.all_gather(attn_pack, "lon", axis=0, tiled=False)
    ff_pack = jnp.concatenate([coarse_expand.T, coarse_reduce], axis=0)
    rings = [[z * 8 + y * 2 + c for y in range(4)] for z in range(2) for c in range(2)]
    ff_all = lax.all_gather(ff_pack, "lon", axis=0, tiled=False, axis_index_groups=rings)
    lon_piece = halo(
        fine_lon_plan, LON_PLAN, fine_field[:, :, :6], fine_field[:, :, -6:], 2, 6, fine_shift_lon, True
    )
    lat_piece = fine_rows(fine_lat_plan, low_rows, high_rows, lon_piece, True)
    half_rows = lat_rows // 2
    half_cols = lon_cols // 2

    mixed_fine = fine_attention(
        offsets, band, fine_field, lon_piece, lat_piece, fine_prenorm[None], fine_triple, fine_bias
    )
    lon_piece = halo(fine_lon_plan, LON_PLAN, mixed_fine, mixed_fine, 2, 6, fine_shift_lon, False)
    lat_piece = fine_rows(fine_lat_plan, mixed_fine, mixed_fine, lon_piece, False)
    fine_state, coarse_own = fine_post(
        offsets, mixed_fine, lon_piece, lat_piece, fine_field, fine_output, fine_midnorm[None],
        fine_expand, fine_reduce, merge_gain[None], merge_weight,
    )
    rows_piece = halo(coarse_lat_plan, LAT_PLAN, coarse_own, coarse_own, 1, 3, fine_shift_lat, True)
    framed = lax.dynamic_slice_in_dim(
        jnp.concatenate([rows_piece, coarse_own, rows_piece], axis=1), 3 + coarse_row, half_rows, axis=1
    )
    mine = lax.dynamic_slice_in_dim(framed, 2 * core, 2, axis=0)
    other = swapped(lax.dynamic_slice_in_dim(framed, 2 - 2 * core, 2, axis=0), 1)
    chip = in_order(core, mine, other)
    chip_piece = halo(coarse_lon_plan, LON_PLAN, chip[0], chip[1], 2, 6, chip_shifted, True)
    mid_framed = coarse_attention(offsets, band, chip, chip_piece, coarse_prenorm[None], attn_all)
    cols_piece = halo(coarse_lon_plan, LON_PLAN, mid_framed, mid_framed, 2, 6, chip_shifted, False)
    spread = jnp.concatenate([cols_piece, mid_framed, cols_piece], axis=2)
    first = 6 - coarse_col
    mine = lax.dynamic_slice_in_dim(spread, first + half_cols * core, half_cols, axis=2)
    other = swapped(
        lax.dynamic_slice_in_dim(spread, first + half_cols * (1 - core), half_cols, axis=2), 1
    )
    levels_all = in_order(core, mine, other).reshape(levels, half_rows, half_cols, 8, 128)
    rows_piece = halo(coarse_lat_plan, LAT_PLAN, levels_all, levels_all, 1, 3, fine_shift_lat, False)
    mid_own = lax.dynamic_slice_in_dim(
        jnp.concatenate([rows_piece, levels_all, rows_piece], axis=1), 3 - coarse_row, half_rows, axis=1
    )
    mid_own = mid_own.reshape(WT, 8, 128)
    across = swapped(mid_own, 8)
    mate = swapped(jnp.stack([mid_own, across]), 1)
    keep, send = coarse_ff(mid_own, across, mate, coarse_midnorm[None], ff_all)
    from_mate = swapped(send, 1)
    from_across = swapped((keep[WT:] + from_mate[WT:].astype(F32)).astype(BF), 8)
    return blend(mid_own, keep, from_mate, from_across, upsample_weight, fine_state)


def solution(mesh):
    placed = (
        P(None, "lat", "lon", None),
        P(),
        P(),
        P(),
        P(),
        P(),
        P(),
        P(),
        P(),
        P(),
        P(),
        P(),
        P(None, "lon"),
        P("lon", None, None),
        P("lon", None),
        P(),
        P(None, "lon"),
        P("lon", None),
        P(),
    )
    return jax.shard_map(
        body,
        mesh=mesh,
        in_specs=placed,
        out_specs=(P(None, "lat", "lon", None), P(None, "lat", "lon", None)),
        check_vma=False,
    )
```

```python
import jax
import jax.numpy as jnp
from jax import lax
from jax.sharding import PartitionSpec as P
from jax.experimental import pallas as pl
from jax.experimental.pallas import tpu as pltpu

BF = jnp.bfloat16
F32 = jnp.float32
EPS = 1e-05
NEG = -1e30
WT = 144
MIB = 1024 * 1024


def full_spec(n, smem=(), hbm=()):
    def space(i):
        return pltpu.SMEM if i in smem else pltpu.HBM if i in hbm else pltpu.VMEM

    return [pl.BlockSpec(memory_space=space(i)) for i in range(n)]


def in_hbm(array):
    return pltpu.with_memory_space_constraint(array, pltpu.HBM)


def norm_rows(x, gain):
    mean = jnp.mean(x, axis=-1, keepdims=True)
    off = x - mean
    var = jnp.mean(off * off, axis=-1, keepdims=True)
    return off * lax.rsqrt(var + EPS) * gain


def dot_nt(a, b):
    return lax.dot_general(a, b, (((1,), (1,)), ((), ())), preferred_element_type=F32)


def dot_nn(a, b):
    return jnp.dot(a, b, preferred_element_type=F32)


def rows_to_tiles(rows, tiles, first):
    count = rows.shape[0]
    for c in range(8):
        tiles[pl.ds(first * 8 + c, count, stride=8), :] = rows[:, 128 * c : 128 * c + 128]


def tiles_to_rows(tiles, first, count):
    return [tiles[pl.ds(first * 8 + c, count, stride=8), :] for c in range(8)]


def attend_group(q, k, v, bias_of, extra, scale, store):
    lane_head = lax.broadcasted_iota(jnp.int32, (WT, 128), 1) // 32
    total = None
    for h in range(4):
        pick = lane_head == h
        qh = jnp.where(pick, q, jnp.zeros_like(q))
        vh = jnp.where(pick, v, jnp.zeros_like(v))
        s = dot_nt(qh, k) * scale + (bias_of(h) + extra)
        top = jnp.max(s, axis=-1, keepdims=True)
        p = jnp.exp(s - top)
        inv = 1.0 / jnp.sum(p, axis=-1, keepdims=True)
        o = dot_nn(p.astype(BF), vh) * inv
        total = o if total is None else total + o
    store(total)


def region_mask(thr):
    def reg(dim):
        t = lax.broadcasted_iota(jnp.int32, (WT, WT), dim)
        return jnp.where(t >= 72, t - 72, t) >= thr

    return jnp.where(reg(0) == reg(1), 0.0, NEG).astype(F32)


def frame_of(shift, window):
    ahead = shift <= window // 2
    return ahead, jnp.where(ahead, shift, shift - window)


def region_start(shift, up, band):
    return jnp.where(band == jnp.where(up, 7, 0), 12 * (6 - shift), 1000)


def fill_frame(up, right, own_ref, lon_ref, lat_ref, ext, ahead):
    lat_row = jnp.where(up == ahead, 15, 0)
    after = right == ahead
    for l in range(4):
        for r in range(12):
            ext[l, 3 + r, 6:18] = own_ref[l, r].astype(F32)
        for r in range(3):
            ext[l, lat_row + r, 6:18] = lat_ref[l, r, 0:12].astype(F32)

    def edge(cols):
        for l in range(4):
            for r in range(12):
                ext[l, 3 + r, cols] = lon_ref[l, r].astype(F32)
            for r in range(3):
                ext[l, lat_row + r, cols] = lat_ref[l, r, 12:18].astype(F32)

    @pl.when(after)
    def _():
        edge(slice(18, 24))

    @pl.when(jnp.logical_not(after))
    def _():
        edge(slice(0, 6))


def fine_attn_kernel(sc_ref, band_ref, own_ref, lon_ref, lat_ref, gain_ref, w_hbm, bias_ref, out_ref, ext, xw, xn, q_s, k_s, v_s, mask_s, o_s, w_ref, sem):
    fetch = pltpu.make_async_copy(w_hbm, w_ref, sem.at[0])
    fetch.start()
    up, first_row = frame_of(sc_ref[0], 6)
    right, first_col = frame_of(sc_ref[1], 12)
    row0 = 3 + first_row
    turn = 18 - first_col
    fill_frame(up, right, own_ref, lon_ref, lat_ref, ext, True)
    for dp in range(2):
        for lr in range(2):
            for a in range(2):
                for b in range(6):
                    row = ((dp * 2 + lr) * 12 + a * 6 + b) * 12
                    full = ext[dp * 2 + a, row0 + lr * 6 + b]
                    xw[row : row + 12] = pltpu.roll(full, turn, 0)[0:12]
    gain = gain_ref[...]
    for i in range(4):
        xn[WT * i : WT * i + WT] = norm_rows(xw[WT * i : WT * i + WT], gain).astype(BF)
    place = lax.broadcasted_iota(jnp.int32, (384, 384), 1)
    source = ((place >> 5) & 3) * 96 + (place >> 7) * 32 + (place & 31)
    order = (lax.broadcasted_iota(jnp.int32, (384, 384), 0) == source).astype(F32).astype(BF)
    fetch.wait()
    for j in range(4):
        cols = slice(128 * j, 128 * j + 128)
        w = dot_nn(w_ref[:, 384 * j : 384 * j + 384], order).astype(BF)
        y = dot_nn(xn[...], w).astype(BF)
        q_s[:, cols] = y[:, 0:128]
        k_s[:, cols] = y[:, 128:256]
        v_s[:, cols] = y[:, 256:384]

    def window(i, _):
        thr = jnp.where(i % 2 == jnp.where(up, 1, 0), region_start(sc_ref[0], up, band_ref[0]), 1000)
        mask_s[...] = region_mask(thr)
        rows = pl.ds(i * WT, WT)
        for j in range(4):
            cols = slice(128 * j, 128 * j + 128)

            def store(total, cols=cols):
                o_s[rows, cols] = total

            attend_group(
                q_s[rows, cols], k_s[rows, cols], v_s[rows, cols],
                lambda h, j=j: bias_ref[4 * j + h], mask_s[...], 32 ** (-0.5), store,
            )
        return 0

    lax.fori_loop(0, 4, window, 0)
    for dp in range(2):
        for lr in range(2):
            for a in range(2):
                for b in range(6):
                    row = ((dp * 2 + lr) * 12 + a * 6 + b) * 12
                    out_ref[dp * 2 + a, lr * 6 + b] = o_s[row : row + 12].astype(BF)


def fine_attention(scalars, band, own, lon, lat, gain, weights, bias):
    return pl.pallas_call(
        fine_attn_kernel,
        out_shape=jax.ShapeDtypeStruct((4, 12, 12, 512), BF),
        in_specs=full_spec(8, (0, 1), (6,)),
        out_specs=pl.BlockSpec(memory_space=pltpu.VMEM),
        scratch_shapes=[
            pltpu.VMEM((4, 18, 24, 512), F32),
            pltpu.VMEM((576, 512), F32),
            pltpu.VMEM((576, 512), BF),
            pltpu.VMEM((576, 512), BF),
            pltpu.VMEM((576, 512), BF),
            pltpu.VMEM((576, 512), BF),
            pltpu.VMEM((WT, WT), F32),
            pltpu.VMEM((576, 512), F32),
            pltpu.VMEM((512, 1536), BF),
            pltpu.SemaphoreType.DMA((1,)),
        ],
        compiler_params=pltpu.CompilerParams(vmem_limit_bytes=20 * MIB),
        name="fine_attention",
    )(scalars, band, own, lon, lat, gain, in_hbm(weights), bias)


def fine_post_kernel(sc_ref, own_ref, lon_ref, lat_ref, x_ref, wo_ref, g_ref, we_ref, wr_hbm, mg_ref, wm_hbm, fs_ref, ci_ref, ext, xf, mf, xp, mp, tiles, wr_ref, wm_ref, sem):
    fetch_reduce = pltpu.make_async_copy(wr_hbm, wr_ref, sem.at[0])
    fetch_merge = pltpu.make_async_copy(wm_hbm, wm_ref, sem.at[1])
    fetch_reduce.start()
    fetch_merge.start()
    up, first_row = frame_of(sc_ref[0], 6)
    right, first_col = frame_of(sc_ref[1], 12)
    r0 = 3 - first_row
    turn = (18 + first_col) % 24
    fill_frame(up, right, own_ref, lon_ref, lat_ref, ext, False)
    for l in range(4):
        for r in range(12):
            own_x = x_ref[l, r].astype(F32)
            for c in range(4):
                xf[c, l, r, 0:12] = own_x[:, 128 * c : 128 * c + 128]
    for l in range(4):
        for r in range(12):
            turned = pltpu.roll(ext[l, r0 + r], turn, 0)[0:16]
            for c in range(4):
                mf[c, l, r] = turned[:, 128 * c : 128 * c + 128]
    for b in range(2):
        for a in range(2):
            for p in range(4):
                for i in range(6):
                    row = (2 * b + a) * WT + p * 36 + i * 6
                    for c in range(4):
                        cs = slice(128 * c, 128 * c + 128)
                        mp[row : row + 6, cs] = mf[c, p, 2 * i + a, pl.ds(b, 6, stride=2), :]
                        xp[row : row + 6, cs] = xf[c, p, 2 * i + a, pl.ds(b, 6, stride=2), :]
    fetch_reduce.wait()
    gain = g_ref[...]

    def block(i, _):
        rows = pl.ds(i * WT, WT)
        att = (xp[rows] + dot_nn(mp[rows].astype(BF), wo_ref[...])).astype(BF).astype(F32)
        xn = norm_rows(att, gain).astype(BF)
        hid = jax.nn.gelu(dot_nn(xn, we_ref[...])).astype(BF)
        fs_ref[i] = (att + dot_nn(hid, wr_ref[...])).astype(BF)
        return 0

    lax.fori_loop(0, 4, block, 0)
    fetch_merge.wait()
    parts = [fs_ref[i].astype(F32) for i in range(4)]
    mean = sum(jnp.sum(v, axis=-1, keepdims=True) for v in parts) * (1.0 / 2048)
    parts = [v - mean for v in parts]
    var = sum(jnp.sum(v * v, axis=-1, keepdims=True) for v in parts) * (1.0 / 2048)
    inv = lax.rsqrt(var + EPS)
    acc = None
    for i in range(4):
        cs = slice(512 * i, 512 * i + 512)
        t = dot_nn((parts[i] * inv * mg_ref[:, cs]).astype(BF), wm_ref[cs, :])
        acc = t if acc is None else acc + t
    rows_to_tiles(acc, tiles, 0)
    ci_ref[...] = tiles[...].reshape(4, 6, 6, 8, 128).astype(BF)


def fine_post(scalars, own, lon, lat, field, wo, gain, we, wr, mg, wm):
    return pl.pallas_call(
        fine_post_kernel,
        out_shape=(jax.ShapeDtypeStruct((4, WT, 512), BF), jax.ShapeDtypeStruct((4, 6, 6, 8, 128), BF)),
        in_specs=full_spec(11, (0,), (8, 10)),
        out_specs=(pl.BlockSpec(memory_space=pltpu.VMEM), pl.BlockSpec(memory_space=pltpu.VMEM)),
        scratch_shapes=[
            pltpu.VMEM((4, 18, 24, 512), F32),
            pltpu.VMEM((4, 4, 12, 16, 128), F32),
            pltpu.VMEM((4, 4, 12, 16, 128), F32),
            pltpu.VMEM((576, 512), F32),
            pltpu.VMEM((576, 512), F32),
            pltpu.VMEM((WT * 8, 128), F32),
            pltpu.VMEM((2048, 512), BF),
            pltpu.VMEM((2048, 1024), BF),
            pltpu.SemaphoreType.DMA((2,)),
        ],
        compiler_params=pltpu.CompilerParams(vmem_limit_bytes=30 * MIB),
        name="fine_post",
    )(scalars, own, lon, lat, field, wo, gain, we, in_hbm(wr), mg, in_hbm(wm))


def coarse_attn_kernel(sc_ref, band_ref, own_ref, next_ref, gain_ref, g_ref, out_ref, ext, tiles, xf, xn, acc, mask_s):
    j = pl.program_id(0)

    @pl.when(j == 0)
    def _():
        right, first_col = frame_of(sc_ref[3], 12)
        up, _ = frame_of(sc_ref[2], 6)
        first = 6 + first_col
        edge = jnp.where(right, 18, 0)
        for a in range(2):
            for half in range(2):
                ext[a, :, 6 + 6 * half : 12 + 6 * half] = own_ref[half, a].astype(F32)
            for b in range(6):
                ext[a, b, pl.ds(edge, 6)] = next_ref[a, b].astype(F32)
        for a in range(2):
            for b in range(6):
                row = (a * 6 + b) * 96
                tiles[row : row + 96] = ext[a, b, pl.ds(first, 12)].reshape(96, 128)
        for c, part in enumerate(tiles_to_rows(tiles, 0, WT)):
            xf[:, 128 * c : 128 * c + 128] = part
        xn[...] = norm_rows(xf[...], gain_ref[...]).astype(BF)
        acc[...] = xf[...]
        mask_s[...] = region_mask(region_start(sc_ref[2], up, band_ref[0]))

    def rows_of(first, count):
        return jnp.concatenate([g_ref[0, first : first + count], g_ref[1, first : first + count]], axis=0)

    x = xn[...]
    q = dot_nt(x, rows_of(0, 64)).astype(BF)
    k = dot_nt(x, rows_of(64, 64)).astype(BF)
    v = dot_nt(x, rows_of(128, 64)).astype(BF)

    def bias_of(h):
        def main(part):
            first = (h % 2) * 256 + part * 128
            halves = [g_ref[h // 2, 272:344, first + 512 * i : first + 512 * i + 128].astype(F32) for i in range(2)]
            return jnp.concatenate(halves, axis=0)

        def tail(part):
            first = (h % 2) * 512 + part * 256
            return g_ref[h // 2, 256:272, first : first + 256].astype(F32)

        edge = jnp.transpose(tail(0) + tail(1))[:WT]
        return jnp.concatenate([main(0) + main(1), edge], axis=1)

    def store(total):
        acc[...] += dot_nn(total.astype(BF), rows_of(192, 64))

    attend_group(q, k, v, bias_of, mask_s[...], 32 ** (-0.5), store)

    @pl.when(j == 7)
    def _():
        rows_to_tiles(acc[...], tiles, 0)
        out_ref[...] = tiles[...].reshape(2, 6, 12, 8, 128).astype(BF)


def coarse_attention(scalars, band, own, ahead, gain, packed):
    vm = lambda: pl.BlockSpec(memory_space=pltpu.VMEM)
    return pl.pallas_call(
        coarse_attn_kernel,
        grid=(8,),
        out_shape=jax.ShapeDtypeStruct((2, 6, 12, 8, 128), BF),
        in_specs=[
            pl.BlockSpec(memory_space=pltpu.SMEM), pl.BlockSpec(memory_space=pltpu.SMEM), vm(), vm(), vm(),
            pl.BlockSpec((2, 344, 1024), lambda j: (j, 0, 0)),
        ],
        out_specs=vm(),
        scratch_shapes=[
            pltpu.VMEM((2, 6, 24, 8, 128), F32),
            pltpu.VMEM((WT * 8, 128), F32),
            pltpu.VMEM((WT, 1024), F32),
            pltpu.VMEM((WT, 1024), BF),
            pltpu.VMEM((WT, 1024), F32),
            pltpu.VMEM((WT, WT), F32),
        ],
        compiler_params=pltpu.CompilerParams(vmem_limit_bytes=56 * MIB, dimension_semantics=("arbitrary",)),
        name="coarse_attention",
    )(scalars, band, own, ahead, gain, packed)


def coarse_ff_kernel(own_ref, across_ref, mate_ref, gain_ref, g_hbm, keep_ref, send_ref, tiles, xn, acc, g_ref, sem):
    fetches = [pltpu.make_async_copy(g_hbm.at[i], g_ref.at[i], sem.at[i]) for i in range(4)]
    for fetch in fetches:
        fetch.start()
    sources = (own_ref[...], across_ref[...], mate_ref[0], mate_ref[1])
    for i, block in enumerate(sources):
        tiles[...] = block.astype(F32).reshape(WT * 8, 128)
        x = jnp.concatenate(tiles_to_rows(tiles, 0, WT), axis=1)
        xn[WT * i : WT * i + WT] = norm_rows(x, gain_ref[...]).astype(BF)
    for half in (1, 0):
        rows = slice(2 * WT * half, 2 * WT * half + 2 * WT)
        for i in range(4):
            if half:
                fetches[i].wait()
            hid = jax.nn.gelu(dot_nt(xn[rows], g_ref[i, 0:256])).astype(BF)
            part = dot_nn(hid, g_ref[i, 256:512])
            if i == 0:
                acc[...] = part
            else:
                acc[...] += part
        if half:
            send_ref[...] = acc[...].astype(BF)
        else:
            keep_ref[...] = acc[...]


def coarse_ff(own, across, mate, gain, packed):
    vm = lambda: pl.BlockSpec(memory_space=pltpu.VMEM)
    return pl.pallas_call(
        coarse_ff_kernel,
        out_shape=(jax.ShapeDtypeStruct((2 * WT, 1024), F32), jax.ShapeDtypeStruct((2 * WT, 1024), BF)),
        in_specs=full_spec(5, (), (4,)),
        out_specs=(vm(), vm()),
        scratch_shapes=[
            pltpu.VMEM((WT * 8, 128), F32),
            pltpu.VMEM((4 * WT, 1024), BF),
            pltpu.VMEM((2 * WT, 1024), F32),
            pltpu.VMEM((4, 512, 1024), BF),
            pltpu.SemaphoreType.DMA((4,)),
        ],
        compiler_params=pltpu.CompilerParams(vmem_limit_bytes=20 * MIB),
        name="coarse_ff",
    )(own, across, mate, gain, in_hbm(packed))


def blend_kernel(mid_ref, keep_ref, mate_ref, across_ref, wu_ref, fs_ref, out_ref, cs_ref, tiles, rows_s, grid_s):
    tiles[...] = mid_ref[...].astype(F32).reshape(WT * 8, 128)
    mid = jnp.concatenate(tiles_to_rows(tiles, 0, WT), axis=1)
    added = keep_ref[0:WT] + mate_ref[0:WT].astype(F32) + across_ref[...].astype(F32)
    rows_s[...] = mid + added
    state = rows_s[...].astype(BF)
    for p in range(4):
        for i in range(6):
            row = p * 36 + i * 6
            cs_ref[p, i] = rows_s[row : row + 6].astype(BF)
    for blk in range(4):
        b, a = blk // 2, blk % 2
        e = dot_nn(state, wu_ref[:, 512 * blk : 512 * blk + 512])
        t = fs_ref[blk].astype(F32) + e
        for p in range(4):
            for i in range(6):
                row = p * 36 + i * 6
                for c in range(4):
                    cs = slice(128 * c, 128 * c + 128)
                    grid_s[c, p, 2 * i + a, pl.ds(b, 6, stride=2), :] = t[row : row + 6, cs]
    for p in range(4):
        for r in range(12):
            for c in range(4):
                out_ref[p, r, :, 128 * c : 128 * c + 128] = grid_s[c, p, r, 0:12].astype(BF)


def blend(mid, keep, mate, across, wu, fs):
    return pl.pallas_call(
        blend_kernel,
        out_shape=(jax.ShapeDtypeStruct((4, 12, 12, 512), BF), jax.ShapeDtypeStruct((4, 6, 6, 1024), BF)),
        in_specs=full_spec(6),
        out_specs=(pl.BlockSpec(memory_space=pltpu.VMEM), pl.BlockSpec(memory_space=pltpu.VMEM)),
        scratch_shapes=[
            pltpu.VMEM((WT * 8, 128), F32),
            pltpu.VMEM((WT, 1024), F32),
            pltpu.VMEM((4, 4, 12, 16, 128), F32),
        ],
        compiler_params=pltpu.CompilerParams(vmem_limit_bytes=20 * MIB),
        name="blend",
    )(mid, keep, mate, across, wu, fs)


WL = 6
WW = 12


def shifted(block, axis, distance):
    devices = range(lax.axis_size(axis))
    route = [((i - distance) % len(devices), i) for i in devices]
    return lax.ppermute(block, axis, route)


def swapped(block, bit):
    return lax.ppermute(block, "lon", [(i, i ^ bit) for i in range(lax.axis_size("lon"))])


def chip_shifted(block, distance):
    count = lax.axis_size("lon")
    return lax.ppermute(block, "lon", [((i - 2 * distance) % count, i) for i in range(count)])


def fine_shift_lon(block, distance):
    return shifted(block, "lon", distance)


def fine_shift_lat(block, distance):
    return shifted(block, "lat", distance)


LAT_PLAN = ((1, 1), (1, 2), (1, 3), (-1, 2), (-1, 1))
LON_PLAN = ((1, 1), (1, 3), (1, 6), (-1, 6), (-1, 3), (-1, 1))


def halo(choice, plan, low, high, dim, full, move, to_frame):
    def branch(side, width):
        def send(edges):
            if side == (1 if to_frame else -1):
                piece = move(lax.slice_in_dim(edges[0], 0, width, axis=dim), -1)
                room = (0, full - width)
            else:
                size = edges[1].shape[dim]
                piece = move(lax.slice_in_dim(edges[1], size - width, size, axis=dim), 1)
                room = (full - width, 0)
            return jnp.pad(piece, [room if i == dim else (0, 0) for i in range(piece.ndim)])

        return send

    return lax.switch(choice, [branch(*entry) for entry in plan], (low, high))


def fine_rows(choice, low, high, piece, to_frame):
    def move(edges, distance):
        return fine_shift_lat(jnp.concatenate(edges, axis=2), distance)

    def branch(side, width):
        def send(pair):
            if side == (1 if to_frame else -1):
                return jnp.pad(move([pair[0][:, :width], pair[2][:, :width]], -1), ((0, 0), (0, 3 - width), (0, 0), (0, 0)))
            return jnp.pad(move([pair[1][:, -width:], pair[2][:, -width:]], 1), ((0, 0), (3 - width, 0), (0, 0), (0, 0)))

        return send

    return lax.switch(choice, [branch(*entry) for entry in LAT_PLAN], (low, high, piece))


def moved_rows(choice, block, to_frame):
    def branch(side, width):
        def send(rows):
            if side == (1 if to_frame else -1):
                return jnp.concatenate([rows[:, width:], fine_shift_lat(rows[:, :width], -1)], axis=1)
            return jnp.concatenate([fine_shift_lat(rows[:, -width:], 1), rows[:, :-width]], axis=1)

        return send

    return lax.switch(choice, [branch(*entry) for entry in LAT_PLAN], block)


def plan_choice(shift, steps):
    return sum((shift >= step).astype(jnp.int32) for step in steps)


def in_order(core, mine, other):
    first = jnp.where(core == 0, mine, other)
    second = jnp.where(core == 0, other, mine)
    return jnp.stack([first, second])


def pack_attention(triple, output, bias):
    wide = triple.shape[0]
    columns = triple.reshape(wide, 2, 3, 32).transpose(2, 1, 3, 0).reshape(192, wide)
    high = lax.reduce_precision(bias, 8, 7)
    both = jnp.stack([high, bias - high], axis=1).astype(BF)
    tail = jnp.pad(both[..., 128:].transpose(3, 0, 1, 2), ((0, 0), (0, 0), (0, 0), (0, 256 - WT)))
    main = both[..., :128].reshape(2, 2, 2, 72, 128).transpose(3, 2, 0, 1, 4)
    return jnp.concatenate([columns, output, tail.reshape(16, 1024), main.reshape(72, 1024)], axis=0)


def body(
    fine_field,
    offsets,
    fine_prenorm,
    fine_triple,
    fine_bias,
    fine_output,
    fine_midnorm,
    fine_expand,
    fine_reduce,
    merge_gain,
    merge_weight,
    coarse_prenorm,
    coarse_triple,
    coarse_bias,
    coarse_output,
    coarse_midnorm,
    coarse_expand,
    coarse_reduce,
    upsample_weight,
):
    levels, lat_rows, lon_cols, channels = fine_field.shape
    lat_count = lax.axis_size("lat")
    lat_index = lax.axis_index("lat")
    fine_lat, fine_lon, coarse_lat, coarse_lon = [jnp.maximum(offsets[i], 1) for i in range(4)]
    band = lat_index.astype(jnp.int32).reshape(1)
    core = lax.axis_index("lon") % 2
    coarse_col = frame_of(coarse_lon, WW)[1]
    fine_lat_plan = plan_choice(fine_lat, (2, 3, 4, 5))
    fine_lon_plan = plan_choice(fine_lon, (2, 4, 7, 9, 11))
    coarse_lat_plan = plan_choice(coarse_lat, (2, 3, 4, 5))
    coarse_lon_plan = plan_choice(coarse_lon, (2, 4, 7, 9, 11))
    attn_pack = pack_attention(coarse_triple, coarse_output, coarse_bias)
    low_rows, high_rows = lax.optimization_barrier((fine_field[:, :3], fine_field[:, -3:]))
    attn_all = lax.all_gather(attn_pack, "lon", axis=0, tiled=False)
    ff_pack = jnp.concatenate([coarse_expand.T, coarse_reduce], axis=0)
    rings = [[z * 8 + y * 2 + c for y in range(4)] for z in range(2) for c in range(2)]
    ff_all = lax.all_gather(ff_pack, "lon", axis=0, tiled=False, axis_index_groups=rings)
    lon_piece = halo(
        fine_lon_plan, LON_PLAN, fine_field[:, :, :6], fine_field[:, :, -6:], 2, 6, fine_shift_lon, True
    )
    lat_piece = fine_rows(fine_lat_plan, low_rows, high_rows, lon_piece, True)
    half_rows = lat_rows // 2
    half_cols = lon_cols // 2

    mixed_fine = fine_attention(
        offsets, band, fine_field, lon_piece, lat_piece, fine_prenorm[None], fine_triple, fine_bias
    )
    lon_piece = halo(fine_lon_plan, LON_PLAN, mixed_fine, mixed_fine, 2, 6, fine_shift_lon, False)
    lat_piece = fine_rows(fine_lat_plan, mixed_fine, mixed_fine, lon_piece, False)
    fine_state, coarse_own = fine_post(
        offsets, mixed_fine, lon_piece, lat_piece, fine_field, fine_output, fine_midnorm[None],
        fine_expand, fine_reduce, merge_gain[None], merge_weight,
    )
    framed = moved_rows(coarse_lat_plan, coarse_own, True)
    mine = lax.dynamic_slice_in_dim(framed, 2 * core, 2, axis=0)
    other = swapped(lax.dynamic_slice_in_dim(framed, 2 - 2 * core, 2, axis=0), 1)
    chip = in_order(core, mine, other)
    chip_piece = halo(coarse_lon_plan, LON_PLAN, chip[0], chip[1], 2, 6, chip_shifted, True)
    mid_framed = coarse_attention(offsets, band, chip, chip_piece, coarse_prenorm[None], attn_all)
    cols_piece = halo(coarse_lon_plan, LON_PLAN, mid_framed, mid_framed, 2, 6, chip_shifted, False)
    spread = jnp.concatenate([cols_piece, mid_framed, cols_piece], axis=2)
    first = 6 - coarse_col
    mine = lax.dynamic_slice_in_dim(spread, first + half_cols * core, half_cols, axis=2)
    other = swapped(
        lax.dynamic_slice_in_dim(spread, first + half_cols * (1 - core), half_cols, axis=2), 1
    )
    levels_all = in_order(core, mine, other).reshape(levels, half_rows, half_cols, 8, 128)
    mid_own = moved_rows(coarse_lat_plan, levels_all, False)
    mid_own = mid_own.reshape(WT, 8, 128)
    across = swapped(mid_own, 8)
    mate = swapped(jnp.stack([mid_own, across]), 1)
    keep, send = coarse_ff(mid_own, across, mate, coarse_midnorm[None], ff_all)
    from_mate = swapped(send, 1)
    from_across = swapped((keep[WT:] + from_mate[WT:].astype(F32)).astype(BF), 8)
    return blend(mid_own, keep, from_mate, from_across, upsample_weight, fine_state)


def solution(mesh):
    placed = (
        P(None, "lat", "lon", None),
        P(),
        P(),
        P(),
        P(),
        P(),
        P(),
        P(),
        P(),
        P(),
        P(),
        P(),
        P(None, "lon"),
        P("lon", None, None),
        P("lon", None),
        P(),
        P(None, "lon"),
        P("lon", None),
        P(),
    )
    return jax.shard_map(
        body,
        mesh=mesh,
        in_specs=placed,
        out_specs=(P(None, "lat", "lon", None), P(None, "lat", "lon", None)),
        check_vma=False,
    )
```
